256 devices in a mesh: fsdp: 32 (over z, y), tensor: 8 (over x, core).
Axes of the slice: x: 4, y: 4, z: 8, core: 2. Of those that a mesh axis runs over, the one named last changes fastest.
Arguments:
- context: bfloat16 [8192, 4096], P('fsdp', 'tensor'), may hold values from -6 to 6
- cotangent: bfloat16 [8192, 8192], P('fsdp', 'tensor'), may hold values from -0.0625 to 0.0625
- block_table: int32 [8, 64], P('tensor'), may hold values from 0 to 63, each once within a row
- left_stat: float32 [8, 64, 256, 256], P('tensor', 'fsdp'), may hold values from -1 to 5, as said below
- right_stat: float32 [8, 64, 256, 256], P('tensor', 'fsdp'), may hold values from -1 to 5, as said below
- root_left: float32 [8, 64, 256, 256], P('tensor', 'fsdp'), may hold values from -1 to 5, as said below
- root_right: float32 [8, 64, 256, 256], P('tensor', 'fsdp'), may hold values from -1 to 5, as said below
- second_moment: float32 [8, 64, 256, 256], P('tensor', 'fsdp'), may hold values from 0.3 to 3
Outputs:
- left_new: float32 [8, 64, 256, 256], P('tensor', 'fsdp')
- right_new: float32 [8, 64, 256, 256], P('tensor', 'fsdp')
- second_new: float32 [8, 64, 256, 256], P('tensor', 'fsdp')
- search_direction: bfloat16 [8, 512, 8192], P('tensor', 'fsdp')
The draws below stay inside these ranges and needn't reach their ends.
Inputs may be any that keep to these rules, and one draw needn't show every extreme that they name: Each row of block_table names every block 0 to 63 once. `left_stat`: symmetric, with positive diagonal. `right_stat`: symmetric, with positive diagonal. `root_left`: symmetric, with positive diagonal. `root_right`: symmetric, with positive diagonal.
All inputs are finite; a program needn't handle non-finite values.
Results may differ from the reference program's by a relative error of at most 0.017.
Values may be sent and summed in bfloat16 or wider, within the bound.
A program may use at most 128 MiB of HBM per device.

```python
import math
import jax
import jax.numpy as jnp
from jax import lax

D = 8192
BLOCK = 256
TOK_DEV = 256
HD = 4096
TOKENS = 8192
BAND = 512
COLB = 32
NBT = 64
N_FSDP = 32
N_TENSOR = 8


def symmetric_blocks(base_key, spread):
    first_key, second_key = jax.random.split(base_key)
    full_shape = (N_TENSOR, NBT, BLOCK, BLOCK)
    jitter = jnp.clip(jax.random.normal(first_key, full_shape, jnp.float32), -3.0, 3.0)
    jitter = (jitter + jnp.swapaxes(jitter, -1, -2)) * (spread / math.sqrt(2.0 * BLOCK))
    log_diag = jax.random.uniform(second_key, full_shape[:-1], jnp.float32, math.log(0.5), math.log(4.0))
    identity = jnp.eye(BLOCK, dtype=jnp.float32)
    return jitter + jnp.exp(log_diag)[..., None] * identity


def draw_left_stat(key, part):
    return symmetric_blocks(jax.random.fold_in(key, 11), 0.5)


def draw_right_stat(key, part):
    return symmetric_blocks(jax.random.fold_in(key, 23), 0.5)


def draw_root_left(key, part):
    return symmetric_blocks(jax.random.fold_in(key, 37), 0.6)


def draw_root_right(key, part):
    return symmetric_blocks(jax.random.fold_in(key, 41), 0.6)


def block_scale(stream_key, shape, cuts, smallest, top_value):
    factor_of = 1.0
    for axis_at, shards_of in cuts:
        heights = jax.random.uniform(jax.random.fold_in(jax.random.fold_in(stream_key, 6), axis_at), (shards_of,), jnp.float32, smallest / len(cuts), top_value / len(cuts))
        factor_of = factor_of * jnp.repeat(jnp.exp(heights), shape[axis_at] // shards_of).reshape((-1,) + (1,) * (len(shape) - 1 - axis_at))
    return factor_of


def scatter_about(own_key, shape, width, bound, shards=(), kind=jnp.bfloat16):
    factor_of = block_scale(own_key, shape, shards, -0.22, 0.18) if shards else 1.0
    result = jax.random.normal(own_key, shape, jnp.float32) * width * factor_of
    return jnp.minimum(jnp.maximum(result, -bound), bound).astype(kind)


def setup_inputs(seed: int = 0) -> dict:
    keys = jax.random.split(jax.random.key(seed), 9)
    context = scatter_about(keys[0], (TOKENS, HD), 1.0, 6.0, ((0, 32), (1, 8)))
    cotangent = scatter_about(keys[1], (TOKENS, D), TOKENS ** -0.5, 0.0625, ((0, 32), (1, 8)))
    block_table = jax.vmap(lambda own: jax.random.permutation(own, NBT))(jax.random.split(keys[2], N_TENSOR)).reshape((N_TENSOR, NBT)).astype(jnp.int32)
    left_stat = draw_left_stat(jax.random.fold_in(keys[8], 71), 0)
    right_stat = draw_right_stat(jax.random.fold_in(keys[8], 71), 0)
    root_left = draw_root_left(jax.random.fold_in(keys[8], 71), 0)
    root_right = draw_root_right(jax.random.fold_in(keys[8], 71), 0)
    second_moment = jnp.clip(jnp.exp(math.log(3.0) - 2.3025851 * jax.random.uniform(keys[7], (N_TENSOR, NBT, BLOCK, BLOCK), jnp.float32) ** block_scale(keys[7], (N_TENSOR, NBT, BLOCK, BLOCK), ((0, 8), (1, 32)), -0.2, 0.2)), 0.3, 3.0)
    return {"context": context, "cotangent": cotangent, "block_table": block_table, "left_stat": left_stat, "right_stat": right_stat, "root_left": root_left, "root_right": root_right, "second_moment": second_moment}


decay_rate = 0.95

def reference(context, cotangent, block_table, left_stat, right_stat, root_left, root_right, second_moment):
    ctx_groups = context.reshape(N_FSDP, TOK_DEV, HD)
    cot_groups = cotangent.reshape(N_FSDP, TOK_DEV, D)

    def add_group(running, inputs):
        partial_sum = jnp.dot(inputs[0].T, inputs[1], preferred_element_type=jnp.float32).astype(jnp.bfloat16)
        partial_sum = lax.optimization_barrier(partial_sum)
        return (running + partial_sum.astype(jnp.float32), None)
    gradient, _ = lax.scan(add_group, jnp.zeros((HD, D), jnp.float32), (ctx_groups, cot_groups))
    natural = gradient.reshape(N_TENSOR, BAND // BLOCK, BLOCK, COLB, BLOCK)
    natural = natural.transpose(0, 1, 3, 2, 4).reshape(N_TENSOR, NBT, BLOCK, BLOCK)
    grads = jnp.take_along_axis(natural, block_table.astype(jnp.int32)[:, :, None, None], axis=1)
    highest = lax.Precision.HIGHEST
    gram_left = jnp.einsum('tsij,tskj->tsik', grads, grads, precision=highest)
    gram_right = jnp.einsum('tsji,tsjk->tsik', grads, grads, precision=highest)
    left_new = decay_rate * left_stat + (1.0 - decay_rate) * gram_left / BLOCK
    right_new = decay_rate * right_stat + (1.0 - decay_rate) * gram_right / BLOCK
    second_new = decay_rate * second_moment + (1.0 - decay_rate) * grads * grads
    adam_step = grads / (jnp.sqrt(second_new) + 1e-08)
    shaped = jnp.einsum('tsij,tsjk->tsik', root_left, grads, precision=highest)
    shaped = jnp.einsum('tsij,tsjk->tsik', shaped, root_right, precision=highest)
    graft_ratio = jnp.sqrt(lax.optimization_barrier(jnp.sum(adam_step * adam_step, axis=(2, 3)))) / jnp.sqrt(lax.optimization_barrier(jnp.sum(shaped * shaped, axis=(2, 3))) + 1e-06)
    direction = (shaped * graft_ratio[:, :, None, None]).astype(jnp.bfloat16)
    band_index = jnp.arange(N_TENSOR).astype(jnp.int32)[:, None]
    placed = jnp.zeros((N_TENSOR, NBT, BLOCK, BLOCK), jnp.bfloat16)
    placed = placed.at[band_index, block_table.astype(jnp.int32)].set(direction)
    placed = placed.reshape(N_TENSOR, BAND // BLOCK, COLB, BLOCK, BLOCK).transpose(0, 1, 3, 2, 4)
    search_direction = placed.reshape(N_TENSOR, BAND, D)
    return (left_new, right_new, second_new, search_direction)
```

```python
import functools

import jax
import jax.numpy as jnp
from jax import lax
from jax.experimental import pallas as pl
from jax.experimental.pallas import tpu as pltpu
from jax.sharding import Mesh
from jax.sharding import PartitionSpec as P

MESH = pl.DeviceIdType.MESH
bf16 = jnp.bfloat16
f32 = jnp.float32
decay_rate = 0.95

NZ, NY, NX = 8, 4, 4
TOK = 256
BLOCK = 256
BAND = 512
COLS = 1024
PATCH = BLOCK // NY
QC = COLS // NY
STRIP = BLOCK // NZ
Y_OFF = (0, -1, 1, 2)
X_OFF = (0, -1, 1, 2)


class Names:
    def __init__(self):
        self.ids = {}

    def __call__(self, *name):
        return self.ids.setdefault(name, len(self.ids))


N_SEND, N_RECV = 160, 128


def kernel(
    ctx, cot, tbl, inv, ls, rs, rl, rr, sm,
    ln, rn, sn, sd,
    pieces, relay, bq, aall, cbuf, zr, summed, out1, in1, grad, dirs, in2, rows,
    ls_v, rs_v, rl_v, rr_v, sm_v,
    send_sems, recv_sems, a1s, a1r, a2s, a2r, loc,
):
    x, y, z, c = (lax.axis_index(n) for n in ("x", "y", "z", "c"))
    me = z * NY + y
    t_me = x * 2 + c
    started = []
    sid, rid = Names(), Names()

    def wrap(v, n):
        return lax.rem(v + n, n)

    def send(src, dst, name, **where):
        k = sid(len(started))
        copy = pltpu.make_async_remote_copy(
            src_ref=src, dst_ref=dst,
            send_sem=send_sems.at[k], recv_sem=recv_sems.at[rid(*name)],
            device_id=where, device_id_type=MESH,
        )
        copy.start()
        started.append(copy)

    def arrived(dst, *name):
        pltpu.make_async_remote_copy(
            src_ref=dst, dst_ref=dst,
            send_sem=send_sems.at[0], recv_sem=recv_sems.at[rid(*name)],
            device_id={"c": 1 - c}, device_id_type=MESH,
        ).wait_recv()

    yp, ym, y2 = wrap(y + 1, NY), wrap(y - 1, NY), wrap(y + 2, NY)
    xp, xm = wrap(x + 1, NX), wrap(x - 1, NX)
    zp, zm = wrap(z + 1, NZ), wrap(z - 1, NZ)

    stats = [
        pltpu.make_async_copy(a, b, loc.at[i])
        for i, (a, b) in enumerate(((rl, rl_v), (rr, rr_v), (sm, sm_v), (ls, ls_v), (rs, rs_v)))
    ]

    barrier = pltpu.get_barrier_semaphore()
    for where in ({"y": yp}, {"y": ym}, {"x": xp}, {"x": xm}, {"z": zp}, {"z": zm}, {"c": 1 - c}):
        pl.semaphore_signal(barrier, inc=1, device_id=where, device_id_type=MESH)

    src_col = lax.broadcasted_iota(jnp.int32, (512, 512), 0)
    q = lax.broadcasted_iota(jnp.int32, (512, 512), 1)
    lane = lax.rem(q, 128)
    y_of = lax.rem(q // 128 + y, NY)
    pick = (src_col == (lane // PATCH) * BLOCK + PATCH * y_of + lax.rem(lane, PATCH)).astype(f32).astype(bf16)
    for j in range(2):
        got = jnp.dot(cot[:, 512 * j : 512 * j + 512], pick, preferred_element_type=f32).astype(bf16)
        for r in range(NY):
            pieces[r, :, 128 * j : 128 * j + 128] = got[:, 128 * r : 128 * r + 128]

    def bpart(t, ya, half=None):
        if half is None:
            return bq.at[t, pl.ds(ya * TOK, TOK)]
        return bq.at[t, pl.ds(ya * TOK + half * (TOK // 2), TOK // 2)]

    pl.semaphore_wait(barrier, 7)

    here = bpart(t_me, y)
    send(pieces.at[1], here, ("By", -1), y=yp)
    send(pieces.at[3], here, ("By", 1), y=ym)
    send(pieces.at[2, pl.ds(0, TOK // 2)], relay.at[0], ("Rb", 0), y=yp)
    send(pieces.at[2, pl.ds(TOK // 2, TOK // 2)], relay.at[1], ("Rb", 1), y=ym)
    send(pieces.at[0], here, ("Bx", -1, 0), x=xp)
    send(pieces.at[0], here, ("Bx", 1, 0), x=xm)
    send(pieces.at[0], here, ("Bc", 0, 0), c=1 - c)
    for copy in stats:
        copy.start()
    bq[t_me, pl.ds(y * TOK, TOK)] = pieces[0]

    turned = ctx[...].astype(f32).T.astype(bf16)
    lanes = pl.ds(pl.multiple_of(y * TOK, TOK), TOK)
    for zz in range(NZ):
        for h in range(2):
            aall[zz * 64 + h * 32 : zz * 64 + h * 32 + 32, lanes] = turned[
                h * 256 + zz * 32 : h * 256 + zz * 32 + 32
            ]

    def apart(ya, half=None):
        cols = pl.ds(pl.multiple_of(ya * TOK, TOK), TOK)
        if half is None:
            return aall.at[:, cols]
        return aall.at[pl.ds(half * 256, 256), cols]

    send(apart(y), apart(y), ("Ay", -1), y=yp)
    send(apart(y), apart(y), ("Ay", 1), y=ym)

    def spread(yi):
        part = bpart(t_me, wrap(y + Y_OFF[yi], NY))
        send(part, part, ("Bx", -1, yi), x=xp)
        send(part, part, ("Bx", 1, yi), x=xm)
        send(part, part, ("Bc", 0, yi), c=1 - c)

    arrived(here, "By", -1)
    spread(1)
    arrived(here, "By", 1)
    spread(2)
    arrived(relay.at[0], "Rb", 0)
    send(relay.at[0], bpart(t_me, ym, 0), ("By2", 0), y=yp)
    arrived(relay.at[1], "Rb", 1)
    send(relay.at[1], bpart(t_me, yp, 1), ("By2", 1), y=ym)

    def pass_on(yi):
        ya = wrap(y + Y_OFF[yi], NY)
        for off, x_at, half, to in ((-1, xm, 0, xp), (1, xp, 1, xm)):
            t = x_at * 2 + c
            arrived(bpart(t, ya), "Bx", off, yi)
            send(bpart(t, ya, half), bpart(t, ya, half), ("Bx2", half, yi), x=to)
            send(bpart(t, ya), bpart(t, ya), ("Bc", off, yi), c=1 - c)

    pass_on(0)
    arrived(bpart(t_me, y2, 0), "By2", 0)
    arrived(bpart(t_me, y2, 1), "By2", 1)
    spread(3)
    arrived(apart(ym), "Ay", -1)
    send(apart(ym, 0), apart(ym, 0), ("Ay2", 0), y=yp)
    arrived(apart(yp), "Ay", 1)
    send(apart(yp, 1), apart(yp, 1), ("Ay2", 1), y=ym)
    pass_on(1)
    pass_on(2)
    arrived(apart(y2, 0), "Ay2", 0)
    arrived(apart(y2, 1), "Ay2", 1)

    def product(g):
        off = X_OFF[g]
        xa = wrap(x + off, NX)
        for yi in range(NY):
            arrived(here, "Bc", off, yi)

        def one(cc, carry):
            total = jnp.dot(aall[...], bq[xa * 2 + cc], preferred_element_type=f32)
            cbuf[g, :, :, pl.ds(pl.multiple_of(cc * QC, QC), QC)] = total.astype(bf16).reshape(NZ, 64, QC)
            return carry

        lax.fori_loop(0, 2, one, 0)

    half_rows = (pl.ds(0, 32), pl.ds(32, 32))

    def step(g, s):
        dist = 5 - s
        for d, sign, to in ((0, 1, zp), (1, -1, zm)):
            zd = wrap(z + sign * dist, NZ)
            name = ("Z", g, d, s)
            if s == 1:
                send(cbuf.at[g, zd, half_rows[d]], zr.at[g, d, 0, half_rows[d]], name, z=to)
                continue
            if s == 2:
                arrived(zr.at[g, d, 0, half_rows[d]], "Z", g, d, 1)
                cbuf[g, zd, half_rows[d]] = (
                    cbuf[g, zd, half_rows[d]].astype(f32) + zr[g, d, 0, half_rows[d]].astype(f32)
                ).astype(bf16)
            else:
                arrived(zr.at[g, d, s - 2], "Z", g, d, s - 1)
                cbuf[g, zd] = (cbuf[g, zd].astype(f32) + zr[g, d, s - 2].astype(f32)).astype(bf16)
            send(cbuf.at[g, zd], zr.at[g, d, s - 1], name, z=to)

    def last(g):
        xa = wrap(x + X_OFF[g], NX)
        arrived(zr.at[g, 0, 3], "Z", g, 0, 4)
        arrived(zr.at[g, 1, 3], "Z", g, 1, 4)
        whole = cbuf[g, z].astype(f32) + zr[g, 0, 3].astype(f32) + zr[g, 1, 3].astype(f32)
        for k in range(4):
            tile = whole[:, 128 * k : 128 * k + 128]
            summed[xa * 4 + k, 0] = tile[:32]
            summed[xa * 4 + k, 1] = tile[32:]

    product(0)
    step(0, 1)
    pass_on(3)
    product(1)
    step(1, 1)
    product(2)
    step(2, 1)
    for g in range(3):
        step(g, 2)
    for yi in range(NY):
        t = wrap(x + 2, NX) * 2 + c
        ya = wrap(y + Y_OFF[yi], NY)
        arrived(bpart(t, ya, 0), "Bx2", 0, yi)
        arrived(bpart(t, ya, 1), "Bx2", 1, yi)
        send(bpart(t, ya), bpart(t, ya), ("Bc", 2, yi), c=1 - c)
    step(0, 3)
    product(3)
    step(3, 1)
    step(1, 3)
    step(2, 3)
    step(3, 2)
    step(0, 4)
    step(1, 4)
    step(2, 4)
    step(3, 3)
    step(3, 4)
    for g in range(4):
        last(g)

    left_lanes = lax.broadcasted_iota(jnp.int32, (16, 128), 1) < 64

    def patches(f, slot_of):
        for s in range(2):
            k = tbl[0, 2 * f + s]
            col = k & 31
            tile = summed[col >> 1, k >> 5]
            odd = (col & 1) == 1
            upper, lower = tile[:16], tile[16:]
            up_turned, low_turned = pltpu.roll(upper, 64, 1), pltpu.roll(lower, 64, 1)
            first = jnp.where(odd, up_turned, upper)
            second = jnp.where(odd, lower, low_turned)
            slot_of(s, jnp.where(left_lanes, first, second).astype(bf16))

    def far_order(i):
        dz, dy = i // NY, lax.rem(i, NY)
        zd = lax.rem(z + dz, NZ)
        yd = lax.rem(y + dy, NY)
        return zd, yd, zd * NY + yd

    def copy1(i):
        zd, yd, f = far_order(i)
        return pltpu.make_async_remote_copy(
            src_ref=out1.at[i], dst_ref=in1.at[me], send_sem=a1s.at[i], recv_sem=a1r.at[i],
            device_id={"z": zd, "y": yd}, device_id_type=MESH,
        )

    def send1(i, carry):
        zd, yd, f = far_order(i)

        def put(s, v):
            out1[i, s] = v

        patches(f, put)
        copy1(i).start()
        return carry

    lax.fori_loop(1, 32, send1, 0)

    def put_own(s, v):
        in1[me, s] = v

    patches(me, put_own)

    def wait1(i, carry):
        copy1(i).wait_recv()
        return carry

    lax.fori_loop(1, 32, wait1, 0)

    for s in range(2):
        for j in range(2):
            for zz in range(NZ):
                a = in1[zz * NY + 2 * j, s].astype(f32)
                b = in1[zz * NY + 2 * j + 1, s].astype(f32)
                at = pl.ds(128 * j, 128)
                grad[s, 32 * zz : 32 * zz + 16, at] = jnp.where(left_lanes, a, pltpu.roll(b, 64, 1))
                grad[s, 32 * zz + 16 : 32 * zz + 32, at] = jnp.where(left_lanes, pltpu.roll(a, 64, 1), b)

    highest = lax.Precision.HIGHEST
    for copy in stats[:3]:
        copy.wait()
    for s in range(2):
        g = grad[s]
        second = decay_rate * sm_v[s] + (1.0 - decay_rate) * g * g
        sm_v[s] = second
        adam = g / (jnp.sqrt(second) + 1e-08)
        shaped = jnp.dot(rl_v[s], g, precision=highest, preferred_element_type=f32)
        shaped = jnp.dot(shaped, rr_v[s], precision=highest, preferred_element_type=f32)
        ratio = jnp.sqrt(jnp.sum(adam * adam, keepdims=True)) / jnp.sqrt(
            jnp.sum(shaped * shaped, keepdims=True) + 1e-06
        )
        dirs[:, s] = (shaped * ratio).astype(bf16).reshape(16, 16, BLOCK)

    def copy2(i):
        zd, yd, f = far_order(i)
        return pltpu.make_async_remote_copy(
            src_ref=dirs.at[lax.rem(f, 16)], dst_ref=in2.at[me], send_sem=a2s.at[i], recv_sem=a2r.at[i],
            device_id={"z": zd, "y": yd}, device_id_type=MESH,
        )

    def send2(i, carry):
        copy2(i).start()
        return carry

    lax.fori_loop(1, 32, send2, 0)
    in2[me] = dirs[lax.rem(me, 16)]

    out_sn = pltpu.make_async_copy(sm_v, sn, loc.at[5])
    out_sn.start()
    for copy in stats[3:]:
        copy.wait()
    for s in range(2):
        g = grad[s].astype(bf16)
        left = lax.dot_general(g, g, (((1,), (1,)), ((), ())), preferred_element_type=f32)
        ls_v[s] = decay_rate * ls_v[s] + (1.0 - decay_rate) * left / BLOCK
        right = lax.dot_general(g, g, (((0,), (0,)), ((), ())), preferred_element_type=f32)
        rs_v[s] = decay_rate * rs_v[s] + (1.0 - decay_rate) * right / BLOCK
    out_ln = pltpu.make_async_copy(ls_v, ln, loc.at[6])
    out_rn = pltpu.make_async_copy(rs_v, rn, loc.at[7])
    out_ln.start()
    out_rn.start()

    def wait2(i, carry):
        copy2(i).wait_recv()
        return carry

    lax.fori_loop(1, 32, wait2, 0)
    half = me // 16
    for col in range(32):
        p = inv[0, half * 32 + col]
        rows[:, BLOCK * col : BLOCK * col + BLOCK] = in2[p >> 1, p & 1]
    out_sd = pltpu.make_async_copy(rows, sd, loc.at[8])
    out_sd.start()

    for copy in started:
        copy.wait_send()

    def drain(i, carry):
        copy1(i).wait_send()
        copy2(i).wait_send()
        return carry

    lax.fori_loop(1, 32, drain, 0)
    for copy in (out_sn, out_ln, out_rn, out_sd):
        copy.wait()


def per_device(context, cotangent, block_table, left_stat, right_stat, root_left, root_right, second_moment):
    ids = jnp.arange(64, dtype=jnp.int32)
    inverse = jnp.sum(jnp.where(block_table[0][None, :] == ids[:, None], ids[None, :], 0), axis=1)[None]
    vmem = pl.BlockSpec(memory_space=pltpu.VMEM)
    smem = pl.BlockSpec(memory_space=pltpu.SMEM)
    hbm = pl.BlockSpec(memory_space=pl.ANY)
    block = jax.ShapeDtypeStruct((2, BLOCK, BLOCK), f32)
    V = pltpu.VMEM
    DMA = pltpu.SemaphoreType.DMA
    ln, rn, sn, sd = pl.pallas_call(
        kernel,
        out_shape=(block, block, block, jax.ShapeDtypeStruct((16, 8192), bf16)),
        in_specs=[vmem, vmem, smem, smem, hbm, hbm, hbm, hbm, hbm],
        out_specs=(hbm, hbm, hbm, hbm),
        scratch_shapes=[
            V((NY, TOK, QC), bf16),
            V((2, TOK // 2, QC), bf16),
            V((8, NY * TOK, QC), bf16),
            V((BAND, NY * TOK), bf16),
            V((4, NZ, 64, 2 * QC), bf16),
            V((4, 2, 4, 64, 2 * QC), bf16),
            V((16, 2, 32, 128), f32),
            V((32, 2, 16, 128), bf16),
            V((32, 2, 16, 128), bf16),
            V((2, BLOCK, BLOCK), f32),
            V((16, 2, 16, BLOCK), bf16),
            V((32, 2, 16, BLOCK), bf16),
            V((16, 8192), bf16),
            *[V((2, BLOCK, BLOCK), f32)] * 5,
            DMA((N_SEND,)),
            DMA((N_RECV,)),
            DMA((32,)),
            DMA((32,)),
            DMA((32,)),
            DMA((32,)),
            DMA((9,)),
        ],
        compiler_params=pltpu.CompilerParams(collective_id=0, has_side_effects=True, vmem_limit_bytes=48 << 20),
        name="shampoo",
    )(
        context, cotangent, block_table, inverse,
        left_stat[0], right_stat[0], root_left[0], root_right[0], second_moment[0],
    )
    return ln[None], rn[None], sn[None], sd[None]


def solution(mesh):
    finer = Mesh(mesh.devices.reshape(NZ, NY, NX, 2), ("z", "y", "x", "c"))
    F, T = ("z", "y"), ("x", "c")
    stat = P(T, F, None, None)
    return jax.shard_map(
        per_device,
        mesh=finer,
        in_specs=(P(F, T), P(F, T), P(T, None), stat, stat, stat, stat, stat),
        out_specs=(stat, stat, stat, P(T, F, None)),
        check_vma=False,
    )
```

```python
import functools

import jax
import jax.numpy as jnp
from jax import lax
from jax.experimental import pallas as pl
from jax.experimental.pallas import tpu as pltpu
from jax.sharding import Mesh
from jax.sharding import PartitionSpec as P

MESH = pl.DeviceIdType.MESH
bf16 = jnp.bfloat16
f32 = jnp.float32
decay_rate = 0.95

NZ, NY, NX = 8, 4, 4
TOK = 256
BLOCK = 256
BAND = 512
COLS = 1024
PATCH = BLOCK // NY
QC = COLS // NY
STRIP = BLOCK // NZ
Y_OFF = (0, -1, 1, 2)
PEER_OFF = (1, -1, 2)
REL = (4, 3, -3, 2, -2, 1, -1, 0)
SETS = ((0, 64), (64, 192), (192, 320), (320, 512))
X_OFF = (0, -1, 1, 2)


class Names:
    def __init__(self):
        self.ids = {}

    def __call__(self, *name):
        return self.ids.setdefault(name, len(self.ids))


N_SEND, N_RECV = 160, 128


def kernel(
    ctx_h, cot_h, tbl, inv, ls, rs, rl, rr, sm,
    ln, rn, sn, sd,
    ctx, cot, turn, pieces, bq, aall, cbuf, zr, summed, out1, in1, grad, dirs, in2, rows,
    ls_v, rs_v, rl_v, rr_v, sm_v,
    send_sems, recv_sems, a1s, a1r, a2s, a2r, loc,
):
    x, y, z, c = (lax.axis_index(n) for n in ("x", "y", "z", "c"))
    me = z * NY + y
    t_me = x * 2 + c
    started = []
    sid, rid = Names(), Names()

    def wrap(v, n):
        return lax.rem(v + n, n)

    def send(src, dst, name, **where):
        k = sid(len(started))
        copy = pltpu.make_async_remote_copy(
            src_ref=src, dst_ref=dst,
            send_sem=send_sems.at[k], recv_sem=recv_sems.at[rid(*name)],
            device_id=where, device_id_type=MESH,
        )
        copy.start()
        started.append(copy)

    def arrived(dst, *name):
        pltpu.make_async_remote_copy(
            src_ref=dst, dst_ref=dst,
            send_sem=send_sems.at[0], recv_sem=recv_sems.at[rid(*name)],
            device_id={"c": 1 - c}, device_id_type=MESH,
        ).wait_recv()

    y_at = {off: wrap(y + off, NY) for off in (0, 1, -1, 2)}
    xp, xm = wrap(x + 1, NX), wrap(x - 1, NX)
    zp, zm = wrap(z + 1, NZ), wrap(z - 1, NZ)

    load_cot = pltpu.make_async_copy(cot_h, cot, loc.at[9])
    load_ctx = pltpu.make_async_copy(ctx_h, ctx, loc.at[10])
    load_cot.start()
    load_ctx.start()
    stats = [
        pltpu.make_async_copy(a, b, loc.at[i])
        for i, (a, b) in enumerate(((rl, rl_v), (rr, rr_v), (sm, sm_v), (ls, ls_v), (rs, rs_v)))
    ]

    barrier = pltpu.get_barrier_semaphore()
    near = [{"y": y_at[off]} for off in PEER_OFF] + [{"x": xp}, {"x": xm}, {"z": zp}, {"z": zm}, {"c": 1 - c}]
    for where in near:
        pl.semaphore_signal(barrier, inc=1, device_id=where, device_id_type=MESH)

    src_col = lax.broadcasted_iota(jnp.int32, (512, 512), 0)
    q = lax.broadcasted_iota(jnp.int32, (512, 512), 1)
    lane = lax.rem(q, 128)
    y_of = lax.rem(q // 128 + y, NY)
    pick = (src_col == (lane // PATCH) * BLOCK + PATCH * y_of + lax.rem(lane, PATCH)).astype(f32).astype(bf16)
    load_cot.wait()
    for j in range(2):
        got = jnp.dot(cot[:, 512 * j : 512 * j + 512], pick, preferred_element_type=f32).astype(bf16)
        for r in range(NY):
            pieces[r, :, 128 * j : 128 * j + 128] = got[:, 128 * r : 128 * r + 128]

    def bpart(t, ya, half=None):
        if half is None:
            return bq.at[t, pl.ds(ya * TOK, TOK)]
        return bq.at[t, pl.ds(ya * TOK + half * (TOK // 2), TOK // 2)]

    pl.semaphore_wait(barrier, len(near))

    here = bpart(t_me, y)
    send(pieces.at[1], here, ("By", -1), y=y_at[1])
    send(pieces.at[3], here, ("By", 1), y=y_at[-1])
    send(pieces.at[0], here, ("Bx", -1, 0), x=xp)
    send(pieces.at[0], here, ("Bx", 1, 0), x=xm)
    send(pieces.at[0], here, ("Bc", 0, 0), c=1 - c)
    for copy in stats:
        copy.start()

    load_ctx.wait()
    turn[...] = ctx[...].astype(f32).T.astype(bf16)
    lanes = pl.ds(pl.multiple_of(y * TOK, TOK), TOK)
    for pos, rel in enumerate(REL):
        zz = wrap(z + rel, NZ)
        for h in range(2):
            aall[pos * 64 + h * 32 : pos * 64 + h * 32 + 32, lanes] = turn[
                pl.ds(pl.multiple_of(h * 256 + zz * 32, 32), 32)
            ]

    def apart(off, k):
        first, end = SETS[k]
        return aall.at[pl.ds(first, end - first), pl.ds(pl.multiple_of(y_at[off] * TOK, TOK), TOK)]

    def send_rows(k):
        for off in PEER_OFF:
            send(apart(0, k), apart(0, k), ("A", k, -off if off != 2 else 2), y=y_at[off])

    send_rows(0)
    send(pieces.at[2], here, ("By", 2), y=y_at[2])
    for k in range(1, len(SETS)):
        send_rows(k)
    bq[t_me, pl.ds(y * TOK, TOK)] = pieces[0]

    def spread(yi):
        part = bpart(t_me, y_at[Y_OFF[yi]])
        arrived(part, "By", Y_OFF[yi])
        send(part, part, ("Bx", -1, yi), x=xp)
        send(part, part, ("Bx", 1, yi), x=xm)
        send(part, part, ("Bc", 0, yi), c=1 - c)

    def pass_on(yi):
        ya = y_at[Y_OFF[yi]]
        for off, x_at, half, to in ((-1, xm, 0, xp), (1, xp, 1, xm)):
            t = x_at * 2 + c
            arrived(bpart(t, ya), "Bx", off, yi)
            send(bpart(t, ya, half), bpart(t, ya, half), ("Bx2", half, yi), x=to)
            send(bpart(t, ya), bpart(t, ya), ("Bc", off, yi), c=1 - c)

    def far(yi):
        t = wrap(x + 2, NX) * 2 + c
        ya = y_at[Y_OFF[yi]]
        arrived(bpart(t, ya, 0), "Bx2", 0, yi)
        arrived(bpart(t, ya, 1), "Bx2", 1, yi)
        send(bpart(t, ya), bpart(t, ya), ("Bc", 2, yi), c=1 - c)

    def rows_here(k):
        for off in PEER_OFF:
            arrived(apart(off, k), "A", k, off)

    def columns_here(u):
        if u % 2:
            for yi in range(NY):
                arrived(here, "Bc", X_OFF[u // 2], yi)

    def piece_of(u):
        xa = wrap(x + X_OFF[u // 2], NX)
        return xa * 2 + (1 - c if u % 2 else c)

    def product(u, k, end=None):
        first = SETS[k][0]
        last_row = SETS[k if end is None else end][1]
        total = jnp.dot(aall[first:last_row], bq[piece_of(u)], preferred_element_type=f32)
        cbuf[u, first // 64 : last_row // 64] = total.astype(bf16).reshape((last_row - first) // 64, 64, QC)

    def step(u, s):
        for d, to in ((0, zp), (1, zm)):
            name = ("Z", u, d, s)
            half = pl.ds(32 * d, 32)
            if s == 1:
                send(cbuf.at[u, 0, half], zr.at[u, d, 0, half], name, z=to)
                continue
            pos = 2 * s - 3 + d
            if s == 2:
                arrived(zr.at[u, d, 0, half], "Z", u, d, 1)
                cbuf[u, pos, half] = (cbuf[u, pos, half].astype(f32) + zr[u, d, 0, half].astype(f32)).astype(bf16)
            else:
                arrived(zr.at[u, d, s - 2], "Z", u, d, s - 1)
                cbuf[u, pos] = (cbuf[u, pos].astype(f32) + zr[u, d, s - 2].astype(f32)).astype(bf16)
            send(cbuf.at[u, pos], zr.at[u, d, s - 1], name, z=to)

    def last(u):
        arrived(zr.at[u, 0, 3], "Z", u, 0, 4)
        arrived(zr.at[u, 1, 3], "Z", u, 1, 4)
        whole = cbuf[u, 7].astype(f32) + zr[u, 0, 3].astype(f32) + zr[u, 1, 3].astype(f32)
        for j in range(2):
            tile = whole[:, 128 * j : 128 * j + 128]
            summed[piece_of(u) * 2 + j, 0] = tile[:32]
            summed[piece_of(u) * 2 + j, 1] = tile[32:]

    def steps(*pairs):
        for u, s in pairs:
            step(u, s)

    spread(1)
    spread(2)
    pass_on(0)
    rows_here(0)
    spread(3)
    product(0, 0)
    step(0, 1)
    columns_here(1)
    product(1, 0)
    step(1, 1)
    pass_on(1)
    pass_on(2)
    rows_here(1)
    for u in (0, 1):
        product(u, 1)
        step(u, 2)
    rows_here(2)
    for u in (0, 1):
        product(u, 2)
        step(u, 3)
    pass_on(3)
    for u in (2, 4, 3, 5):
        columns_here(u)
        product(u, 0, 2)
        step(u, 1)
    rows_here(3)
    for u in (0, 1):
        product(u, 3)
        step(u, 4)
    for yi in range(NY - 1):
        far(yi)
    for u in (2, 4, 3, 5):
        product(u, 3)
        step(u, 2)
    far(3)
    for u in (6, 7):
        columns_here(u)
        product(u, 0, 3)
        step(u, 1)
    steps((2, 3), (4, 3), (3, 3), (5, 3))
    last(0)
    last(1)
    steps((6, 2), (7, 2), (2, 4), (4, 4), (6, 3), (7, 3), (3, 4), (5, 4), (6, 4), (7, 4))
    for u in (2, 4, 3, 5, 6, 7):
        last(u)

    left_lanes = lax.broadcasted_iota(jnp.int32, (16, 128), 1) < 64

    def patch(f, s):
        k = tbl[0, 2 * f + s]
        col = k & 31
        tile = summed[col >> 1, k >> 5]
        odd = (col & 1) == 1
        upper, lower = tile[:16], tile[16:]
        first = jnp.where(odd, pltpu.roll(upper, 64, 1), upper)
        second = jnp.where(odd, lower, pltpu.roll(lower, 64, 1))
        return jnp.where(left_lanes, first, second).astype(bf16)

    def other(i):
        k = i // NY
        dz = 4 + ((k + 1) // 2) * (1 - 2 * lax.rem(k, 2))
        zd = lax.rem(z + dz, NZ)
        yd = lax.rem(y + 3 - lax.rem(i, NY), NY)
        return zd, yd, zd * NY + yd

    def copy1(i, s):
        zd, yd, f = other(i)
        return pltpu.make_async_remote_copy(
            src_ref=out1.at[s, i], dst_ref=in1.at[s, me], send_sem=a1s.at[s, i], recv_sem=a1r.at[s, i],
            device_id={"z": zd, "y": yd}, device_id_type=MESH,
        )

    def copy2(i, s):
        zd, yd, f = other(i)
        return pltpu.make_async_remote_copy(
            src_ref=dirs.at[s, lax.rem(f, 16)], dst_ref=in2.at[s, me], send_sem=a2s.at[s, i], recv_sem=a2r.at[s, i],
            device_id={"z": zd, "y": yd}, device_id_type=MESH,
        )

    def each(do):
        def body(i, carry):
            do(i)
            return carry

        lax.fori_loop(0, 31, body, 0)

    for s in range(2):

        def send1(i, s=s):
            f = other(i)[2]
            out1[s, i] = patch(f, s)
            copy1(i, s).start()

        each(send1)
        in1[s, me] = patch(me, s)

    highest = lax.Precision.HIGHEST
    for copy in stats[:3]:
        copy.wait()
    out_sn = []
    for s in range(2):
        each(lambda i, s=s: copy1(i, s).wait_recv())
        for j in range(2):
            for zz in range(NZ):
                a = in1[s, zz * NY + 2 * j].astype(f32)
                b = in1[s, zz * NY + 2 * j + 1].astype(f32)
                at = pl.ds(128 * j, 128)
                grad[s, 32 * zz : 32 * zz + 16, at] = jnp.where(left_lanes, a, pltpu.roll(b, 64, 1))
                grad[s, 32 * zz + 16 : 32 * zz + 32, at] = jnp.where(left_lanes, pltpu.roll(a, 64, 1), b)
        g = grad[s]
        second = decay_rate * sm_v[s] + (1.0 - decay_rate) * g * g
        sm_v[s] = second
        adam = g / (jnp.sqrt(second) + 1e-08)
        shaped = jnp.dot(rl_v[s], g, precision=highest, preferred_element_type=f32)
        shaped = jnp.dot(shaped, rr_v[s], precision=highest, preferred_element_type=f32)
        ratio = jnp.sqrt(jnp.sum(adam * adam, keepdims=True)) / jnp.sqrt(
            jnp.sum(shaped * shaped, keepdims=True) + 1e-06
        )
        dirs[s] = (shaped * ratio).astype(bf16).reshape(16, 16, BLOCK)
        each(lambda i, s=s: copy2(i, s).start())
        in2[s, me] = dirs[s, lax.rem(me, 16)]

    out_sn = pltpu.make_async_copy(sm_v, sn, loc.at[5])
    out_sn.start()
    for copy in stats[3:]:
        copy.wait()
    for s in range(2):
        g = grad[s].astype(bf16)
        left = lax.dot_general(g, g, (((1,), (1,)), ((), ())), preferred_element_type=f32)
        ls_v[s] = decay_rate * ls_v[s] + (1.0 - decay_rate) * left / BLOCK
        right = lax.dot_general(g, g, (((0,), (0,)), ((), ())), preferred_element_type=f32)
        rs_v[s] = decay_rate * rs_v[s] + (1.0 - decay_rate) * right / BLOCK
    out_ln = pltpu.make_async_copy(ls_v, ln, loc.at[6])
    out_rn = pltpu.make_async_copy(rs_v, rn, loc.at[7])
    out_ln.start()
    out_rn.start()

    for copy in started:
        copy.wait_send()
    for s in range(2):
        each(lambda i, s=s: copy1(i, s).wait_send())
    for s in range(2):
        each(lambda i, s=s: copy2(i, s).wait_recv())
    half = me // 16
    for col in range(32):
        p = inv[0, half * 32 + col]
        rows[:, BLOCK * col : BLOCK * col + BLOCK] = in2[p & 1, p >> 1]
    out_sd = pltpu.make_async_copy(rows, sd, loc.at[8])
    out_sd.start()
    for s in range(2):
        each(lambda i, s=s: copy2(i, s).wait_send())
    for copy in (out_sn, out_ln, out_rn, out_sd):
        copy.wait()


def per_device(context, cotangent, block_table, left_stat, right_stat, root_left, root_right, second_moment):
    ids = jnp.arange(64, dtype=jnp.int32)
    inverse = jnp.sum(jnp.where(block_table[0][None, :] == ids[:, None], ids[None, :], 0), axis=1)[None]
    smem = pl.BlockSpec(memory_space=pltpu.SMEM)
    hbm = pl.BlockSpec(memory_space=pltpu.HBM)
    block = jax.ShapeDtypeStruct((2, BLOCK, BLOCK), f32)
    V = pltpu.VMEM
    DMA = pltpu.SemaphoreType.DMA
    ln, rn, sn, sd = pl.pallas_call(
        kernel,
        out_shape=(block, block, block, jax.ShapeDtypeStruct((16, 8192), bf16)),
        in_specs=[hbm, hbm, smem, smem, hbm, hbm, hbm, hbm, hbm],
        out_specs=(hbm, hbm, hbm, hbm),
        scratch_shapes=[
            V((TOK, BAND), bf16),
            V((TOK, COLS), bf16),
            V((BAND, TOK), bf16),
            V((NY, TOK, QC), bf16),
            V((8, NY * TOK, QC), bf16),
            V((BAND, NY * TOK), bf16),
            V((8, NZ, 64, QC), bf16),
            V((8, 2, 4, 64, QC), bf16),
            V((16, 2, 32, 128), f32),
            V((2, 32, 16, 128), bf16),
            V((2, 32, 16, 128), bf16),
            V((2, BLOCK, BLOCK), f32),
            V((2, 16, 16, BLOCK), bf16),
            V((2, 32, 16, BLOCK), bf16),
            V((16, 8192), bf16),
            *[V((2, BLOCK, BLOCK), f32)] * 5,
            DMA((N_SEND,)),
            DMA((N_RECV,)),
            DMA((2, 32)),
            DMA((2, 32)),
            DMA((2, 32)),
            DMA((2, 32)),
            DMA((11,)),
        ],
        compiler_params=pltpu.CompilerParams(collective_id=0, has_side_effects=True, vmem_limit_bytes=67_043_328),
        name="shampoo",
    )(
        context, cotangent, block_table, inverse,
        left_stat[0], right_stat[0], root_left[0], root_right[0], second_moment[0],
    )
    return ln[None], rn[None], sn[None], sd[None]


def solution(mesh):
    finer = Mesh(mesh.devices.reshape(NZ, NY, NX, 2), ("z", "y", "x", "c"))
    F, T = ("z", "y"), ("x", "c")
    stat = P(T, F, None, None)
    return jax.shard_map(
        per_device,
        mesh=finer,
        in_specs=(P(F, T), P(F, T), P(T, None), stat, stat, stat, stat, stat),
        out_specs=(stat, stat, stat, P(T, F, None)),
        check_vma=False,
    )
```

```python
import functools

import jax
import jax.numpy as jnp
from jax import lax
from jax.experimental import pallas as pl
from jax.experimental.pallas import tpu as pltpu
from jax.sharding import Mesh
from jax.sharding import PartitionSpec as P

MESH = pl.DeviceIdType.MESH
bf16 = jnp.bfloat16
f32 = jnp.float32
decay_rate = 0.95

NZ, NY, NX = 8, 4, 4
TOK = 256
BLOCK = 256
BAND = 512
COLS = 1024
PATCH = BLOCK // NY
QC = COLS // NY
STRIP = BLOCK // NZ
Y_OFF = (0, -1, 1, 2)
PEER_OFF = (1, -1, 2)
REL = (4, 3, -3, 2, -2, 1, -1, 0)
SETS = ((0, 64), (64, 192), (192, 320), (320, 512))
X_OFF = (0, -1, 1, 2)

PLAN = (
    ("first",), ("xd", 0, 0), ("turn",), ("yq", "A", 0), ("yq", "B2", 0), ("yq", "A", 1), ("yq", "A", 2),
    ("yq", "A", 3), ("sp", 1, 0), ("sp", 2, 0), ("got", 0, 0, -1), ("got", 0, 0, 1), ("sp", 3, 0),
    ("pr", 0, 0, 0, 0), ("z", 0, 0, 1, 0), ("z", 0, 0, 1, 1), ("pr", 1, 0, 0, 0), ("z", 1, 0, 1, 0),
    ("z", 1, 0, 1, 1), ("got", 1, 0, -1), ("got", 1, 0, 1), ("rel", 1, 0, 0), ("rel", 1, 0, 1), ("far", 0, 0),
    ("pr", 0, 0, 1, 1), ("z", 0, 0, 2, 0), ("z", 0, 0, 2, 1), ("pr", 1, 0, 1, 1), ("z", 1, 0, 2, 0),
    ("z", 1, 0, 2, 1), ("got", 2, 0, -1), ("got", 2, 0, 1), ("rel", 2, 0, 0), ("rel", 2, 0, 1), ("pr", 0, 0, 2, 2),
    ("z", 0, 0, 3, 0), ("z", 0, 0, 3, 1), ("pr", 1, 0, 2, 2), ("z", 1, 0, 3, 0), ("z", 1, 0, 3, 1),
    ("got", 3, 0, -1), ("got", 3, 0, 1), ("rel", 3, 0, 0), ("rel", 3, 0, 1), ("pr", 2, 0, 0, 2), ("z", 2, 0, 1, 0),
    ("z", 2, 0, 1, 1), ("pr", 4, 0, 0, 2), ("z", 4, 0, 1, 0), ("z", 4, 0, 1, 1), ("far", 1, 0), ("pr", 3, 0, 0, 2),
    ("z", 3, 0, 1, 0), ("z", 3, 0, 1, 1), ("pr", 5, 0, 0, 2), ("z", 5, 0, 1, 0), ("z", 5, 0, 1, 1),
    ("pr", 0, 0, 3, 3), ("z", 0, 0, 4, 0), ("z", 0, 0, 4, 1), ("pr", 1, 0, 3, 3), ("z", 1, 0, 4, 0),
    ("z", 1, 0, 4, 1), ("far", 2, 0), ("z", 2, 0, 2, 0), ("z", 2, 0, 2, 1), ("z", 4, 0, 2, 0), ("z", 4, 0, 2, 1),
    ("far", 3, 0), ("z", 3, 0, 2, 0), ("z", 3, 0, 2, 1), ("z", 5, 0, 2, 0), ("z", 5, 0, 2, 1), ("pr", 6, 0, 0, 3),
    ("z", 6, 0, 1, 0), ("z", 6, 0, 1, 1), ("pr", 7, 0, 0, 3), ("z", 7, 0, 1, 0), ("z", 7, 0, 1, 1),
    ("pr", 2, 0, 3, 3), ("z", 2, 0, 3, 0), ("z", 2, 0, 3, 1), ("pr", 4, 0, 3, 3), ("z", 4, 0, 3, 0),
    ("z", 4, 0, 3, 1), ("pr", 3, 0, 3, 3), ("z", 3, 0, 3, 0), ("z", 3, 0, 3, 1), ("pr", 5, 0, 3, 3),
    ("z", 5, 0, 3, 0), ("z", 5, 0, 3, 1), ("last", 0, 0), ("last", 1, 0), ("z", 6, 0, 2, 0), ("z", 6, 0, 2, 1),
    ("z", 7, 0, 2, 0), ("z", 7, 0, 2, 1), ("z", 2, 0, 4, 0), ("z", 2, 0, 4, 1), ("z", 4, 0, 4, 0), ("z", 4, 0, 4, 1),
    ("z", 6, 0, 3, 0), ("z", 6, 0, 3, 1), ("z", 7, 0, 3, 0), ("z", 7, 0, 3, 1), ("z", 3, 0, 4, 0), ("z", 3, 0, 4, 1),
    ("z", 5, 0, 4, 0), ("z", 5, 0, 4, 1), ("z", 6, 0, 4, 0), ("z", 6, 0, 4, 1), ("z", 7, 0, 4, 0), ("z", 7, 0, 4, 1),
    ("last", 2, 0), ("last", 4, 0), ("last", 3, 0), ("last", 5, 0), ("last", 6, 0), ("last", 7, 0),
)


class Names:

    def __init__(self):
        self.ids = {}

    def __call__(self, *name):
        return self.ids.setdefault(name, len(self.ids))


N_SEND = N_RECV = 320
PARTS = 1
HALF = QC // PARTS
STRAIGHT = (0,)
TWO = ()


def kernel(
    ctx_h, cot_h, tbl, ls, rs, rl, rr, sm,
    ln, rn, sn, in2,
    ctx, cot, turn, pieces, bq, aall, cbuf, zr, summed, out1, in1, grad, dirs,
    ls_v, rs_v, rl_v, rr_v, sm_v,
    send_sems, recv_sems, a1s, a1r, a2s, a2r, loc,
):
    x, y, z, c = (lax.axis_index(n) for n in ("x", "y", "z", "c"))
    me = z * NY + y
    t_me = x * 2 + c
    started = []
    waited = set()
    rid = Names()

    def wrap(v, n):
        return lax.rem(v + n, n)

    def send(src, dst, name, **where):
        copy = pltpu.make_async_remote_copy(
            src_ref=src, dst_ref=dst,
            send_sem=send_sems.at[len(started)], recv_sem=recv_sems.at[rid(*name)],
            device_id=where, device_id_type=MESH,
        )
        copy.start()
        started.append(copy)

    def need(dst, *name):
        if name in waited:
            return
        waited.add(name)
        pltpu.make_async_remote_copy(
            src_ref=dst, dst_ref=dst,
            send_sem=send_sems.at[0], recv_sem=recv_sems.at[rid(*name)],
            device_id={"c": 1 - c}, device_id_type=MESH,
        ).wait_recv()

    y_at = {off: wrap(y + off, NY) for off in (0, 1, -1, 2)}
    x_at = {off: wrap(x + off, NX) for off in (0, 1, -1, 2)}
    z_to = (wrap(z + 1, NZ), wrap(z - 1, NZ))
    z_two = (wrap(z + 2, NZ), wrap(z - 2, NZ))

    load_cot = pltpu.make_async_copy(cot_h, cot, loc.at[8])
    load_ctx = pltpu.make_async_copy(ctx_h, ctx, loc.at[9])
    load_cot.start()
    load_ctx.start()
    stats = [
        pltpu.make_async_copy(a, b, loc.at[i])
        for i, (a, b) in enumerate(((rl, rl_v), (rr, rr_v), (sm, sm_v), (ls, ls_v), (rs, rs_v)))
    ]

    barrier = pltpu.get_barrier_semaphore()
    near = [{"x": x_at[2]}] + [{"z": v} for v in z_two] + [{"y": y_at[off]} for off in PEER_OFF] + [{"x": x_at[1]}, {"x": x_at[-1]}]
    near += [{"z": z_to[0]}, {"z": z_to[1]}, {"c": 1 - c}]
    for where in near:
        pl.semaphore_signal(barrier, inc=1, device_id=where, device_id_type=MESH)

    src_col = lax.broadcasted_iota(jnp.int32, (512, 512), 0)
    q = lax.broadcasted_iota(jnp.int32, (1, 512), 1)
    from_col = (((q & 127) >> 6) << 8) + ((((q >> 7) + y) & 3) << 6) + (q & 63)
    pick = (src_col == from_col).astype(f32).astype(bf16)
    load_cot.wait()
    for j in range(2):
        got = jnp.dot(cot[:, 512 * j : 512 * j + 512], pick, preferred_element_type=f32).astype(bf16)
        for r in range(NY):
            at = pl.ds(j % (2 // PARTS) * 128, 128)
            pieces[r, j * PARTS // 2, :, at] = got[:, 128 * r : 128 * r + 128]

    def bpart(t, j, ya, half=None):
        if half is None:
            return bq.at[t, j, pl.ds(ya * TOK, TOK)]
        return bq.at[t, j, pl.ds(ya * TOK + half * (TOK // 2), TOK // 2)]

    def apart(off, k, half=None):
        first, end = SETS[k]
        size = end - first
        if half is not None:
            size //= 2
            first += half * size
        return aall.at[pl.ds(first, size), pl.ds(pl.multiple_of(y_at[off] * TOK, TOK), TOK)]

    def send_by(j):
        send(pieces.at[1, j], bpart(t_me, j, y), ("By", -1, j), y=y_at[1])
        send(pieces.at[3, j], bpart(t_me, j, y), ("By", 1, j), y=y_at[-1])

    def send_pieces(src, part, yi, j):
        send(src, part, ("Bx", -1, yi, j), x=x_at[1])
        send(src, part, ("Bx", 1, yi, j), x=x_at[-1])
        send(src, part, ("Bc", 0, yi, j), c=1 - c)

    def first():
        send_by(0)
        for j in range(PARTS):
            send_pieces(pieces.at[0, j], bpart(t_me, j, y), 0, j)
        for copy in stats:
            copy.start()

    def turned():
        load_ctx.wait()
        turn[...] = ctx[...].astype(f32).T.astype(bf16)
        lanes = pl.ds(pl.multiple_of(y * TOK, TOK), TOK)
        for pos, rel in enumerate(REL):
            zz = wrap(z + rel, NZ)
            for h in range(2):
                aall[pos * 64 + h * 32 : pos * 64 + h * 32 + 32, lanes] = turn[
                    pl.ds(pl.multiple_of(h * 256 + zz * 32, 32), 32)
                ]
        for j in range(PARTS):
            bq[t_me, j, pl.ds(y * TOK, TOK)] = pieces[0, j]

    def over_y(what, k):
        if what == "A":
            send(apart(0, k), apart(0, k), ("A", k, -1), y=y_at[1])
            send(apart(0, k), apart(0, k), ("A", k, 1), y=y_at[-1])
            send(apart(0, k), apart(0, k), ("A", k, 2), y=y_at[2])
        elif what == "By":
            send_by(k)
        else:
            send(pieces.at[2, k], bpart(t_me, k, y), ("By", 2, k), y=y_at[2])

    def pass_rows(k, h):
        off = 2 * h - 1
        need(apart(off, k), "A", k, off)
        send(apart(off, k, h), apart(off, k, h), ("A2", k, h), y=y_at[-off])

    def from_y(yi, j):
        need(bpart(t_me, j, y_at[Y_OFF[yi]]), "By", Y_OFF[yi], j)

    def spread(yi, j):
        from_y(yi, j)
        part = bpart(t_me, j, y_at[Y_OFF[yi]])
        send_pieces(part, part, yi, j)

    def x_part(off, yi, j, half=None):
        return bpart(x_at[off] * 2 + c, j, y_at[Y_OFF[yi]], half)

    def from_x(off, yi, j):
        if off == 2:
            if yi in STRAIGHT:
                need(x_part(2, yi, j), "Bx2", 0, yi, j)
                return
            for h in range(2):
                need(x_part(2, yi, j, h), "Bx2", h, yi, j)
        else:
            need(x_part(off, yi, j), "Bx", off, yi, j)

    def share(yi, j, off):
        from_x(off, yi, j)
        send(x_part(off, yi, j), x_part(off, yi, j), ("Bc", off, yi, j), c=1 - c)

    def relay(yi, j, h):
        off = 2 * h - 1
        from_x(off, yi, j)
        send(x_part(off, yi, j, h), x_part(off, yi, j, h), ("Bx2", h, yi, j), x=x_at[-off])

    def straight(yi, j):
        if yi:
            from_y(yi, j)
        src = bpart(t_me, j, y_at[Y_OFF[yi]]) if yi else pieces.at[0, j]
        send(src, bpart(t_me, j, y_at[Y_OFF[yi]]), ("Bx2", 0, yi, j), x=x_at[2])

    def piece_of(u):
        return x_at[X_OFF[u // 2]] * 2 + (1 - c if u % 2 else c)

    def product(u, j, k, end):
        off = X_OFF[u // 2]
        for yi in range(NY):
            if u % 2:
                need(bpart(t_me, j, y), "Bc", off, yi, j)
            elif off:
                from_x(off, yi, j)
            elif yi:
                from_y(yi, j)
        for kk in range(k, end + 1):
            for off in (-1, 1):
                need(apart(off, kk), "A", kk, off)
            need(apart(2, kk), "A", kk, 2)
        r0, r1 = SETS[k][0], SETS[end][1]
        total = jnp.dot(aall[r0:r1], bq[piece_of(u), j], preferred_element_type=f32)
        cbuf[u, j, r0 // 64 : r1 // 64] = total.astype(bf16).reshape((r1 - r0) // 64, 64, HALF)

    def step(u, j, s, d):
        name = ("Z", u, j, d, s)
        half = pl.ds(32 * d, 32)
        if s == 1:
            send(cbuf.at[u, j, 0, half], zr.at[u, j, d, 0, half], name, z=z_to[d])
            return
        pos = 2 * s - 3 + d
        if s == 2:
            need(zr.at[u, j, d, 0, half], "Z", u, j, d, 1)
            cbuf[u, j, pos, half] = (
                cbuf[u, j, pos, half].astype(f32) + zr[u, j, d, 0, half].astype(f32)
            ).astype(bf16)
        else:
            need(zr.at[u, j, d, s - 2], "Z", u, j, d, s - 1)
            cbuf[u, j, pos] = (cbuf[u, j, pos].astype(f32) + zr[u, j, d, s - 2].astype(f32)).astype(bf16)
        send(cbuf.at[u, j, pos], zr.at[u, j, d, s - 1], name, z=z_to[d])

    def two_start(u, j):
        for d in range(2):
            half = pl.ds(32 * d, 32)
            send(cbuf.at[u, j, 0, half], zr.at[u, j, d, 0, half], ("Z", u, j, d, 1), z=z_two[d])
            send(cbuf.at[u, j, 1 + d], zr.at[u, j, d, 1], ("Z", u, j, d, 2), z=z_to[d])

    def two_near(u, j):
        for d in range(2):
            send(cbuf.at[u, j, 5 + d], zr.at[u, j, d, 3], ("Z", u, j, d, 4), z=z_to[d])

    def two_end(u, j):
        for d in range(2):
            half = pl.ds(32 * d, 32)
            need(zr.at[u, j, d, 0, half], "Z", u, j, d, 1)
            need(zr.at[u, j, d, 1], "Z", u, j, d, 2)
            for h in range(2):
                at = pl.ds(32 * h, 32)
                part = cbuf[u, j, 3 + d, at].astype(f32) + zr[u, j, d, 1, at].astype(f32)
                if h == d:
                    part += zr[u, j, d, 0, at].astype(f32)
                cbuf[u, j, 3 + d, at] = part.astype(bf16)
            send(cbuf.at[u, j, 3 + d], zr.at[u, j, d, 2], ("Z", u, j, d, 3), z=z_two[d])

    def last(u, j):
        whole = cbuf[u, j, 7].astype(f32)
        for d in range(2):
            need(zr.at[u, j, d, 3], "Z", u, j, d, 4)
            whole += zr[u, j, d, 3].astype(f32)
            if u in TWO:
                need(zr.at[u, j, d, 2], "Z", u, j, d, 3)
                whole += zr[u, j, d, 2].astype(f32)
        for i in range(2 // PARTS):
            tile = whole[:, 128 * i : 128 * i + 128]
            summed[piece_of(u) * 2 + j + i, 0] = tile[:32]
            summed[piece_of(u) * 2 + j + i, 1] = tile[32:]

    pl.semaphore_wait(barrier, len(near))
    acts = {
        "first": first, "turn": turned, "yq": over_y, "rr": pass_rows, "sp": spread, "got": share, "rel": relay, "xd": straight,
        "far": lambda yi, j: share(yi, j, 2), "pr": product, "z": step, "last": last,
        "za": two_start, "zb": two_end, "zc": two_near,
    }
    for act, *rest in PLAN:
        acts[act](*rest)

    left_lanes = lax.broadcasted_iota(jnp.int32, (16, 128), 1) < 64

    def patch(f, s):
        k = tbl[0, 2 * f + s]
        col = k & 31
        tile = summed[col >> 1, k >> 5]
        odd = (col & 1) == 1
        upper, lower = tile[:16], tile[16:]
        first = jnp.where(odd, pltpu.roll(upper, 64, 1), upper)
        second = jnp.where(odd, lower, pltpu.roll(lower, 64, 1))
        return jnp.where(left_lanes, first, second).astype(bf16)

    def other(i):
        k = i // NY
        dz = 4 + ((k + 1) // 2) * (1 - 2 * lax.rem(k, 2))
        zd = lax.rem(z + dz, NZ)
        yd = lax.rem(y + 3 - lax.rem(i, NY), NY)
        return zd, yd, zd * NY + yd

    def copy1(i, s):
        zd, yd, f = other(i)
        return pltpu.make_async_remote_copy(
            src_ref=out1.at[s, i], dst_ref=in1.at[s, me], send_sem=a1s.at[s, i], recv_sem=a1r.at[s, i],
            device_id={"z": zd, "y": yd}, device_id_type=MESH,
        )

    def copy2(i, s):
        zd, yd, f = other(i)
        return pltpu.make_async_remote_copy(
            src_ref=dirs.at[s, lax.rem(f, 16)], dst_ref=in2.at[s, me], send_sem=a2s.at[s, i], recv_sem=a2r.at[s, i],
            device_id={"z": zd, "y": yd}, device_id_type=MESH,
        )

    def each(do):
        def body(k, carry):
            for i in range(NY):
                do(k * NY + i)
            return carry

        lax.fori_loop(0, NZ - 1, body, 0)
        for i in range(NY * (NZ - 1), NY * NZ - 1):
            do(i)

    for s in range(2):

        def send1(k, carry, s=s, dests=NY):
            for i in range(dests):
                out1[s, k * NY + i] = patch(other(k * NY + i)[2], s)
            for i in range(dests):
                copy1(k * NY + i, s).start()
            return carry

        lax.fori_loop(0, NZ - 1, send1, 0)
        send1(NZ - 1, 0, dests=NY - 1)
        in1[s, me] = patch(me, s)

    highest = lax.Precision.HIGHEST
    for copy in stats[:3]:
        copy.wait()
    own = [pltpu.make_async_copy(dirs.at[s, lax.rem(me, 16)], in2.at[s, me], loc.at[10 + s]) for s in range(2)]
    for s in range(2):
        each(lambda i, s=s: copy1(i, s).wait_recv())
        for j in range(2):
            for zz in range(NZ):
                a = in1[s, zz * NY + 2 * j].astype(f32)
                b = in1[s, zz * NY + 2 * j + 1].astype(f32)
                at = pl.ds(128 * j, 128)
                grad[s, 32 * zz : 32 * zz + 16, at] = jnp.where(left_lanes, a, pltpu.roll(b, 64, 1))
                grad[s, 32 * zz + 16 : 32 * zz + 32, at] = jnp.where(left_lanes, pltpu.roll(a, 64, 1), b)
        g = grad[s]
        second = decay_rate * sm_v[s] + (1.0 - decay_rate) * g * g
        sm_v[s] = second
        adam = g / (jnp.sqrt(second) + 1e-08)
        shaped = jnp.dot(rl_v[s], g, precision=highest, preferred_element_type=f32)
        shaped = jnp.dot(shaped, rr_v[s], precision=highest, preferred_element_type=f32)
        ratio = jnp.sqrt(jnp.sum(adam * adam, keepdims=True)) / jnp.sqrt(
            jnp.sum(shaped * shaped, keepdims=True) + 1e-06
        )
        dirs[s] = (shaped * ratio).astype(bf16).reshape(16, 16, BLOCK)
        each(lambda i, s=s: copy2(i, s).start())
        own[s].start()

    out_sn = pltpu.make_async_copy(sm_v, sn, loc.at[5])
    out_sn.start()
    for copy in stats[3:]:
        copy.wait()
    for s in range(2):
        g = grad[s].astype(bf16)
        left = lax.dot_general(g, g, (((1,), (1,)), ((), ())), preferred_element_type=f32)
        ls_v[s] = decay_rate * ls_v[s] + (1.0 - decay_rate) * left / BLOCK
        right = lax.dot_general(g, g, (((0,), (0,)), ((), ())), preferred_element_type=f32)
        rs_v[s] = decay_rate * rs_v[s] + (1.0 - decay_rate) * right / BLOCK
    out_ln = pltpu.make_async_copy(ls_v, ln, loc.at[6])
    out_rn = pltpu.make_async_copy(rs_v, rn, loc.at[7])
    out_ln.start()
    out_rn.start()

    for copy in started:
        copy.wait_send()
    for s in range(2):
        each(lambda i, s=s: copy1(i, s).wait_send())
    for s in range(2):
        each(lambda i, s=s: copy2(i, s).wait_recv())
    for s in range(2):
        each(lambda i, s=s: copy2(i, s).wait_send())
    for copy in (out_sn, out_ln, out_rn, *own):
        copy.wait()


def emit(tbl, ln_i, rn_i, sn_i, in2, ln, rn, sn, sd, ln_v, rn_v, sn_v, strips, rows, inv, sems):
    half = (lax.axis_index("z") * NY + lax.axis_index("y")) // 16
    load = pltpu.make_async_copy(in2, strips, sems.at[3])
    load.start()
    whole = ((ln_i, ln_v, ln), (rn_i, rn_v, rn), (sn_i, sn_v, sn))
    for i, (a, b, _) in enumerate(whole):
        pltpu.make_async_copy(a, b, sems.at[i]).start()
    for p in range(64):
        inv[tbl[0, p]] = p
    load.wait()
    for col in range(32):
        p = inv[half * 32 + col]
        rows[:, BLOCK * col : BLOCK * col + BLOCK] = strips[p & 1, p >> 1]
    last = pltpu.make_async_copy(rows, sd, sems.at[3])
    last.start()
    for i, (a, b, o) in enumerate(whole):
        pltpu.make_async_copy(a, b, sems.at[i]).wait()
        pltpu.make_async_copy(b, o, sems.at[i]).start()
    for i, (a, b, o) in enumerate(whole):
        pltpu.make_async_copy(b, o, sems.at[i]).wait()
    last.wait()


def per_device(context, cotangent, block_table, left_stat, right_stat, root_left, root_right, second_moment):
    smem = pl.BlockSpec(memory_space=pltpu.SMEM)
    hbm = pl.BlockSpec(memory_space=pl.ANY)
    block = jax.ShapeDtypeStruct((2, BLOCK, BLOCK), f32)
    V = pltpu.VMEM
    DMA = pltpu.SemaphoreType.DMA
    *new, strips = pl.pallas_call(
        kernel,
        out_shape=(block, block, block, jax.ShapeDtypeStruct((2, 32, 16, BLOCK), bf16)),
        in_specs=[hbm, hbm, smem, hbm, hbm, hbm, hbm, hbm],
        out_specs=(hbm, hbm, hbm, hbm),
        scratch_shapes=[
            V((TOK, BAND), bf16),
            V((TOK, COLS), bf16),
            V((BAND, TOK), bf16),
            V((NY, PARTS, TOK, HALF), bf16),
            V((8, PARTS, NY * TOK, HALF), bf16),
            V((BAND, NY * TOK), bf16),
            V((8, PARTS, NZ, 64, HALF), bf16),
            V((8, PARTS, 2, 4, 64, HALF), bf16),
            V((16, 2, 32, 128), f32),
            V((2, 32, 16, 128), bf16),
            V((2, 32, 16, 128), bf16),
            V((2, BLOCK, BLOCK), f32),
            V((2, 16, 16, BLOCK), bf16),
            *[V((2, BLOCK, BLOCK), f32)] * 5,
            DMA((N_SEND,)),
            DMA((N_RECV,)),
            DMA((2, 32)),
            DMA((2, 32)),
            DMA((2, 32)),
            DMA((2, 32)),
            DMA((12,)),
        ],
        compiler_params=pltpu.CompilerParams(collective_id=0, has_side_effects=True, vmem_limit_bytes=67_043_328),
        name="shampoo",
    )(
        context, cotangent, block_table,
        left_stat[0], right_stat[0], root_left[0], root_right[0], second_moment[0],
    )
    ln, rn, sn, sd = pl.pallas_call(
        emit,
        out_shape=(block, block, block, jax.ShapeDtypeStruct((16, 8192), bf16)),
        in_specs=[smem, hbm, hbm, hbm, hbm],
        out_specs=(hbm, hbm, hbm, hbm),
        scratch_shapes=[
            *[V((2, BLOCK, BLOCK), f32)] * 3,
            V((2, 32, 16, BLOCK), bf16),
            V((16, 8192), bf16),
            pltpu.SMEM((64,), jnp.int32),
            DMA((4,)),
        ],
        compiler_params=pltpu.CompilerParams(vmem_limit_bytes=67_043_328),
        name="emit",
    )(block_table, *new, strips)
    return ln[None], rn[None], sn[None], sd[None]


def solution(mesh):
    finer = Mesh(mesh.devices.reshape(NZ, NY, NX, 2), ("z", "y", "x", "c"))
    F, T = ("z", "y"), ("x", "c")
    stat = P(T, F, None, None)
    return jax.shard_map(
        per_device,
        mesh=finer,
        in_specs=(P(F, T), P(F, T), P(T, None), stat, stat, stat, stat, stat),
        out_specs=(stat, stat, stat, P(T, F, None)),
        check_vma=False,
    )
```

```python
import functools

import jax
import jax.numpy as jnp
from jax import lax
from jax.experimental import pallas as pl
from jax.experimental.pallas import tpu as pltpu
from jax.sharding import Mesh
from jax.sharding import PartitionSpec as P

MESH = pl.DeviceIdType.MESH
bf16 = jnp.bfloat16
f32 = jnp.float32
decay_rate = 0.95

NZ, NY, NX = 8, 4, 4
TOK = 256
BLOCK = 256
BAND = 512
COLS = 1024
PATCH = BLOCK // NY
QC = COLS // NY
STRIP = BLOCK // NZ
Y_OFF = (0, -1, 1, 2)
PEER_OFF = (1, -1, 2)
REL = (4, 3, -3, 2, -2, 1, -1, 0)
SETS = ((0, 64), (64, 192), (192, 320), (320, 512))
X_OFF = (0, -1, 1, 2)


class Names:
    def __init__(self):
        self.ids = {}

    def __call__(self, *name):
        return self.ids.setdefault(name, len(self.ids))


N_SEND, N_RECV = 160, 128


def kernel(
    ctx_h, cot_h, tbl, inv, ls, rs, rl, rr, sm,
    ln, rn, sn, sd,
    ctx, cot, turn, pieces, bq, aall, cbuf, zr, summed, out1, in1, grad, dirs, in2, rows,
    ls_v, rs_v, rl_v, rr_v, sm_v,
    send_sems, recv_sems, a1s, a1r, a2s, a2r, loc,
):
    x, y, z, c = (lax.axis_index(n) for n in ("x", "y", "z", "c"))
    me = z * NY + y
    t_me = x * 2 + c
    started = []
    sid, rid = Names(), Names()

    def wrap(v, n):
        return lax.rem(v + n, n)

    def send(src, dst, name, **where):
        k = sid(len(started))
        copy = pltpu.make_async_remote_copy(
            src_ref=src, dst_ref=dst,
            send_sem=send_sems.at[k], recv_sem=recv_sems.at[rid(*name)],
            device_id=where, device_id_type=MESH,
        )
        copy.start()
        started.append(copy)

    def arrived(dst, *name):
        pltpu.make_async_remote_copy(
            src_ref=dst, dst_ref=dst,
            send_sem=send_sems.at[0], recv_sem=recv_sems.at[rid(*name)],
            device_id={"c": 1 - c}, device_id_type=MESH,
        ).wait_recv()

    y_at = {off: wrap(y + off, NY) for off in (0, 1, -1, 2)}
    xp, xm = wrap(x + 1, NX), wrap(x - 1, NX)
    zp, zm = wrap(z + 1, NZ), wrap(z - 1, NZ)

    load_cot = pltpu.make_async_copy(cot_h, cot, loc.at[9])
    load_ctx = pltpu.make_async_copy(ctx_h, ctx, loc.at[10])
    load_cot.start()
    load_ctx.start()
    stats = [
        pltpu.make_async_copy(a, b, loc.at[i])
        for i, (a, b) in enumerate(((rl, rl_v), (rr, rr_v), (sm, sm_v), (ls, ls_v), (rs, rs_v)))
    ]

    barrier = pltpu.get_barrier_semaphore()
    near = [{"y": y_at[off]} for off in PEER_OFF] + [{"x": xp}, {"x": xm}, {"z": zp}, {"z": zm}, {"c": 1 - c}]
    for where in near:
        pl.semaphore_signal(barrier, inc=1, device_id=where, device_id_type=MESH)

    src_col = lax.broadcasted_iota(jnp.int32, (512, 512), 0)
    q = lax.broadcasted_iota(jnp.int32, (512, 512), 1)
    lane = lax.rem(q, 128)
    y_of = lax.rem(q // 128 + y, NY)
    pick = (src_col == (lane // PATCH) * BLOCK + PATCH * y_of + lax.rem(lane, PATCH)).astype(f32).astype(bf16)
    load_cot.wait()
    for j in range(2):
        got = jnp.dot(cot[:, 512 * j : 512 * j + 512], pick, preferred_element_type=f32).astype(bf16)
        for r in range(NY):
            pieces[r, :, 128 * j : 128 * j + 128] = got[:, 128 * r : 128 * r + 128]

    def bpart(t, ya, half=None):
        if half is None:
            return bq.at[t, pl.ds(ya * TOK, TOK)]
        return bq.at[t, pl.ds(ya * TOK + half * (TOK // 2), TOK // 2)]

    pl.semaphore_wait(barrier, len(near))

    here = bpart(t_me, y)
    send(pieces.at[1], here, ("By", -1), y=y_at[1])
    send(pieces.at[3], here, ("By", 1), y=y_at[-1])
    send(pieces.at[0], here, ("Bx", -1, 0), x=xp)
    send(pieces.at[0], here, ("Bx", 1, 0), x=xm)
    send(pieces.at[0], here, ("Bc", 0, 0), c=1 - c)
    for copy in stats:
        copy.start()

    load_ctx.wait()
    turn[...] = ctx[...].astype(f32).T.astype(bf16)
    lanes = pl.ds(pl.multiple_of(y * TOK, TOK), TOK)
    for pos, rel in enumerate(REL):
        zz = wrap(z + rel, NZ)
        for h in range(2):
            aall[pos * 64 + h * 32 : pos * 64 + h * 32 + 32, lanes] = turn[
                pl.ds(pl.multiple_of(h * 256 + zz * 32, 32), 32)
            ]

    def apart(off, k):
        first, end = SETS[k]
        return aall.at[pl.ds(first, end - first), pl.ds(pl.multiple_of(y_at[off] * TOK, TOK), TOK)]

    def send_rows(k):
        for off in PEER_OFF:
            send(apart(0, k), apart(0, k), ("A", k, -off if off != 2 else 2), y=y_at[off])

    send_rows(0)
    send(pieces.at[2], here, ("By", 2), y=y_at[2])
    for k in range(1, len(SETS)):
        send_rows(k)
    bq[t_me, pl.ds(y * TOK, TOK)] = pieces[0]

    def spread(yi):
        part = bpart(t_me, y_at[Y_OFF[yi]])
        arrived(part, "By", Y_OFF[yi])
        send(part, part, ("Bx", -1, yi), x=xp)
        send(part, part, ("Bx", 1, yi), x=xm)
        send(part, part, ("Bc", 0, yi), c=1 - c)

    def pass_on(yi):
        ya = y_at[Y_OFF[yi]]
        for off, x_at, half, to in ((-1, xm, 0, xp), (1, xp, 1, xm)):
            t = x_at * 2 + c
            arrived(bpart(t, ya), "Bx", off, yi)
            send(bpart(t, ya, half), bpart(t, ya, half), ("Bx2", half, yi), x=to)
            send(bpart(t, ya), bpart(t, ya), ("Bc", off, yi), c=1 - c)

    def far(yi):
        t = wrap(x + 2, NX) * 2 + c
        ya = y_at[Y_OFF[yi]]
        arrived(bpart(t, ya, 0), "Bx2", 0, yi)
        arrived(bpart(t, ya, 1), "Bx2", 1, yi)
        send(bpart(t, ya), bpart(t, ya), ("Bc", 2, yi), c=1 - c)

    def rows_here(k):
        for off in PEER_OFF:
            arrived(apart(off, k), "A", k, off)

    def columns_here(u):
        if u % 2:
            for yi in range(NY):
                arrived(here, "Bc", X_OFF[u // 2], yi)

    def piece_of(u):
        xa = wrap(x + X_OFF[u // 2], NX)
        return xa * 2 + (1 - c if u % 2 else c)

    def product(u, k, end=None):
        first = SETS[k][0]
        last_row = SETS[k if end is None else end][1]
        total = jnp.dot(aall[first:last_row], bq[piece_of(u)], preferred_element_type=f32)
        cbuf[u, first // 64 : last_row // 64] = total.astype(bf16).reshape((last_row - first) // 64, 64, QC)

    def step(u, s):
        for d, to in ((0, zp), (1, zm)):
            name = ("Z", u, d, s)
            half = pl.ds(32 * d, 32)
            if s == 1:
                send(cbuf.at[u, 0, half], zr.at[u, d, 0, half], name, z=to)
                continue
            pos = 2 * s - 3 + d
            if s == 2:
                arrived(zr.at[u, d, 0, half], "Z", u, d, 1)
                cbuf[u, pos, half] = (cbuf[u, pos, half].astype(f32) + zr[u, d, 0, half].astype(f32)).astype(bf16)
            else:
                arrived(zr.at[u, d, s - 2], "Z", u, d, s - 1)
                cbuf[u, pos] = (cbuf[u, pos].astype(f32) + zr[u, d, s - 2].astype(f32)).astype(bf16)
            send(cbuf.at[u, pos], zr.at[u, d, s - 1], name, z=to)

    def last(u):
        arrived(zr.at[u, 0, 3], "Z", u, 0, 4)
        arrived(zr.at[u, 1, 3], "Z", u, 1, 4)
        whole = cbuf[u, 7].astype(f32) + zr[u, 0, 3].astype(f32) + zr[u, 1, 3].astype(f32)
        for j in range(2):
            tile = whole[:, 128 * j : 128 * j + 128]
            summed[piece_of(u) * 2 + j, 0] = tile[:32]
            summed[piece_of(u) * 2 + j, 1] = tile[32:]

    def steps(*pairs):
        for u, s in pairs:
            step(u, s)

    spread(1)
    spread(2)
    pass_on(0)
    rows_here(0)
    spread(3)
    product(0, 0)
    step(0, 1)
    columns_here(1)
    product(1, 0)
    step(1, 1)
    pass_on(1)
    pass_on(2)
    rows_here(1)
    for u in (0, 1):
        product(u, 1)
        step(u, 2)
    rows_here(2)
    for u in (0, 1):
        product(u, 2)
        step(u, 3)
    pass_on(3)
    for u in (2, 4, 3, 5):
        columns_here(u)
        product(u, 0, 2)
        step(u, 1)
    rows_here(3)
    for u in (0, 1):
        product(u, 3)
        step(u, 4)
    for yi in range(NY - 1):
        far(yi)
    for u in (2, 4, 3, 5):
        product(u, 3)
        step(u, 2)
    far(3)
    for u in (6, 7):
        columns_here(u)
        product(u, 0, 3)
        step(u, 1)
    steps((2, 3), (4, 3), (3, 3), (5, 3))
    last(0)
    last(1)
    steps((6, 2), (7, 2), (2, 4), (4, 4), (6, 3), (7, 3), (3, 4), (5, 4), (6, 4), (7, 4))
    for u in (2, 4, 3, 5, 6, 7):
        last(u)

    left_lanes = lax.broadcasted_iota(jnp.int32, (16, 128), 1) < 64

    def patch(f, s):
        k = tbl[0, 2 * f + s]
        col = k & 31
        tile = summed[col >> 1, k >> 5]
        odd = (col & 1) == 1
        upper, lower = tile[:16], tile[16:]
        first = jnp.where(odd, pltpu.roll(upper, 64, 1), upper)
        second = jnp.where(odd, lower, pltpu.roll(lower, 64, 1))
        return jnp.where(left_lanes, first, second).astype(bf16)

    def other(i):
        k = i // NY
        dz = 4 + ((k + 1) // 2) * (1 - 2 * lax.rem(k, 2))
        zd = lax.rem(z + dz, NZ)
        yd = lax.rem(y + 3 - lax.rem(i, NY), NY)
        return zd, yd, zd * NY + yd

    def copy1(i, s):
        zd, yd, f = other(i)
        return pltpu.make_async_remote_copy(
            src_ref=out1.at[s, i], dst_ref=in1.at[s, me], send_sem=a1s.at[s, i], recv_sem=a1r.at[s, i],
            device_id={"z": zd, "y": yd}, device_id_type=MESH,
        )

    def copy2(i, s):
        zd, yd, f = other(i)
        return pltpu.make_async_remote_copy(
            src_ref=dirs.at[s, lax.rem(f, 16)], dst_ref=in2.at[s, me], send_sem=a2s.at[s, i], recv_sem=a2r.at[s, i],
            device_id={"z": zd, "y": yd}, device_id_type=MESH,
        )

    def each(do):
        def body(k, carry):
            for i in range(NY):
                do(k * NY + i)
            return carry

        lax.fori_loop(0, NZ - 1, body, 0)
        for i in range(NY * (NZ - 1), NY * NZ - 1):
            do(i)

    for s in range(2):

        def send1(k, carry, s=s, dests=NY):
            for i in range(dests):
                out1[s, k * NY + i] = patch(other(k * NY + i)[2], s)
            for i in range(dests):
                copy1(k * NY + i, s).start()
            return carry

        lax.fori_loop(0, NZ - 1, send1, 0)
        send1(NZ - 1, 0, dests=NY - 1)
        in1[s, me] = patch(me, s)

    highest = lax.Precision.HIGHEST
    for copy in stats[:3]:
        copy.wait()
    out_sn = []
    for s in range(2):
        each(lambda i, s=s: copy1(i, s).wait_recv())
        for j in range(2):
            for zz in range(NZ):
                a = in1[s, zz * NY + 2 * j].astype(f32)
                b = in1[s, zz * NY + 2 * j + 1].astype(f32)
                at = pl.ds(128 * j, 128)
                grad[s, 32 * zz : 32 * zz + 16, at] = jnp.where(left_lanes, a, pltpu.roll(b, 64, 1))
                grad[s, 32 * zz + 16 : 32 * zz + 32, at] = jnp.where(left_lanes, pltpu.roll(a, 64, 1), b)
        g = grad[s]
        second = decay_rate * sm_v[s] + (1.0 - decay_rate) * g * g
        sm_v[s] = second
        adam = g / (jnp.sqrt(second) + 1e-08)
        shaped = jnp.dot(rl_v[s], g, precision=highest, preferred_element_type=f32)
        shaped = jnp.dot(shaped, rr_v[s], precision=highest, preferred_element_type=f32)
        ratio = jnp.sqrt(jnp.sum(adam * adam, keepdims=True)) / jnp.sqrt(
            jnp.sum(shaped * shaped, keepdims=True) + 1e-06
        )
        dirs[s] = (shaped * ratio).astype(bf16).reshape(16, 16, BLOCK)
        each(lambda i, s=s: copy2(i, s).start())
        in2[s, me] = dirs[s, lax.rem(me, 16)]

    out_sn = pltpu.make_async_copy(sm_v, sn, loc.at[5])
    out_sn.start()
    for copy in stats[3:]:
        copy.wait()
    for s in range(2):
        g = grad[s].astype(bf16)
        left = lax.dot_general(g, g, (((1,), (1,)), ((), ())), preferred_element_type=f32)
        ls_v[s] = decay_rate * ls_v[s] + (1.0 - decay_rate) * left / BLOCK
        right = lax.dot_general(g, g, (((0,), (0,)), ((), ())), preferred_element_type=f32)
        rs_v[s] = decay_rate * rs_v[s] + (1.0 - decay_rate) * right / BLOCK
    out_ln = pltpu.make_async_copy(ls_v, ln, loc.at[6])
    out_rn = pltpu.make_async_copy(rs_v, rn, loc.at[7])
    out_ln.start()
    out_rn.start()

    for copy in started:
        copy.wait_send()
    for s in range(2):
        each(lambda i, s=s: copy1(i, s).wait_send())
    for s in range(2):
        each(lambda i, s=s: copy2(i, s).wait_recv())
    half = me // 16
    for col in range(32):
        p = inv[0, half * 32 + col]
        rows[:, BLOCK * col : BLOCK * col + BLOCK] = in2[p & 1, p >> 1]
    out_sd = pltpu.make_async_copy(rows, sd, loc.at[8])
    out_sd.start()
    for s in range(2):
        each(lambda i, s=s: copy2(i, s).wait_send())
    for copy in (out_sn, out_ln, out_rn, out_sd):
        copy.wait()


def emit(*refs):
    ins, outs, held, sems = refs[:4], refs[4:8], refs[8:12], refs[12]
    for i in range(4):
        pltpu.make_async_copy(ins[i], held[i], sems.at[i]).start()
    for i in range(4):
        pltpu.make_async_copy(ins[i], held[i], sems.at[i]).wait()
        pltpu.make_async_copy(held[i], outs[i], sems.at[i]).start()
    for i in range(4):
        pltpu.make_async_copy(held[i], outs[i], sems.at[i]).wait()


def per_device(context, cotangent, block_table, left_stat, right_stat, root_left, root_right, second_moment):
    ids = jnp.arange(64, dtype=jnp.int32)
    inverse = jnp.sum(jnp.where(block_table[0][None, :] == ids[:, None], ids[None, :], 0), axis=1)[None]
    smem = pl.BlockSpec(memory_space=pltpu.SMEM)
    hbm = pl.BlockSpec(memory_space=pltpu.HBM)
    block = jax.ShapeDtypeStruct((2, BLOCK, BLOCK), f32)
    V = pltpu.VMEM
    DMA = pltpu.SemaphoreType.DMA
    shapes = (block, block, block, jax.ShapeDtypeStruct((16, 8192), bf16))
    made = pl.pallas_call(
        kernel,
        out_shape=(block, block, block, jax.ShapeDtypeStruct((16, 8192), bf16)),
        in_specs=[hbm, hbm, smem, smem, hbm, hbm, hbm, hbm, hbm],
        out_specs=(hbm, hbm, hbm, hbm),
        scratch_shapes=[
            V((TOK, BAND), bf16),
            V((TOK, COLS), bf16),
            V((BAND, TOK), bf16),
            V((NY, TOK, QC), bf16),
            V((8, NY * TOK, QC), bf16),
            V((BAND, NY * TOK), bf16),
            V((8, NZ, 64, QC), bf16),
            V((8, 2, 4, 64, QC), bf16),
            V((16, 2, 32, 128), f32),
            V((2, 32, 16, 128), bf16),
            V((2, 32, 16, 128), bf16),
            V((2, BLOCK, BLOCK), f32),
            V((2, 16, 16, BLOCK), bf16),
            V((2, 32, 16, BLOCK), bf16),
            V((16, 8192), bf16),
            *[V((2, BLOCK, BLOCK), f32)] * 5,
            DMA((N_SEND,)),
            DMA((N_RECV,)),
            DMA((2, 32)),
            DMA((2, 32)),
            DMA((2, 32)),
            DMA((2, 32)),
            DMA((11,)),
        ],
        compiler_params=pltpu.CompilerParams(collective_id=0, has_side_effects=True, vmem_limit_bytes=67_043_328),
        name="shampoo",
    )(
        context, cotangent, block_table, inverse,
        left_stat[0], right_stat[0], root_left[0], root_right[0], second_moment[0],
    )
    ln, rn, sn, sd = pl.pallas_call(
        emit,
        out_shape=shapes,
        in_specs=[hbm] * 4,
        out_specs=(hbm,) * 4,
        scratch_shapes=[*[V(v.shape, v.dtype) for v in shapes], DMA((4,))],
        compiler_params=pltpu.CompilerParams(vmem_limit_bytes=67_043_328),
        name="emit",
    )(*made)
    return ln[None], rn[None], sn[None], sd[None]


def solution(mesh):
    finer = Mesh(mesh.devices.reshape(NZ, NY, NX, 2), ("z", "y", "x", "c"))
    F, T = ("z", "y"), ("x", "c")
    stat = P(T, F, None, None)
    return jax.shard_map(
        per_device,
        mesh=finer,
        in_specs=(P(F, T), P(F, T), P(T, None), stat, stat, stat, stat, stat),
        out_specs=(stat, stat, stat, P(T, F, None)),
        check_vma=False,
    )
```

```python
import functools

import jax
import jax.numpy as jnp
from jax import lax
from jax.experimental import pallas as pl
from jax.experimental.pallas import tpu as pltpu
from jax.sharding import Mesh
from jax.sharding import PartitionSpec as P

MESH = pl.DeviceIdType.MESH
bf16 = jnp.bfloat16
f32 = jnp.float32
decay_rate = 0.95

NZ, NY, NX = 8, 4, 4
TOK = 256
BLOCK = 256
BAND = 512
COLS = 1024
PATCH = BLOCK // NY
QC = COLS // NY
STRIP = BLOCK // NZ
Y_OFF = (0, -1, 1, 2)
PEER_OFF = (1, -1, 2)
REL = (4, 3, -3, 2, -2, 1, -1, 0)
SETS = ((0, 64), (64, 192), (192, 320), (320, 512))
X_OFF = (0, -1, 1, 2)


class Names:
    def __init__(self):
        self.ids = {}

    def __call__(self, *name):
        return self.ids.setdefault(name, len(self.ids))


N_SEND, N_RECV = 160, 128


def kernel(
    ctx_h, cot_h, tbl, inv, ls, rs, rl, rr, sm,
    ln, rn, sn, sd,
    ctx, cot, turn, pieces, bq, aall, cbuf, zr, summed, out1, in1, grad, dirs, in2, rows,
    ls_v, rs_v, rl_v, rr_v, sm_v,
    send_sems, recv_sems, a1s, a1r, a2s, a2r, loc,
):
    x, y, z, c = (lax.axis_index(n) for n in ("x", "y", "z", "c"))
    me = z * NY + y
    t_me = x * 2 + c
    started = []
    sid, rid = Names(), Names()

    def wrap(v, n):
        return lax.rem(v + n, n)

    def send(src, dst, name, **where):
        k = sid(len(started))
        copy = pltpu.make_async_remote_copy(
            src_ref=src, dst_ref=dst,
            send_sem=send_sems.at[k], recv_sem=recv_sems.at[rid(*name)],
            device_id=where, device_id_type=MESH,
        )
        copy.start()
        started.append(copy)

    def arrived(dst, *name):
        pltpu.make_async_remote_copy(
            src_ref=dst, dst_ref=dst,
            send_sem=send_sems.at[0], recv_sem=recv_sems.at[rid(*name)],
            device_id={"c": 1 - c}, device_id_type=MESH,
        ).wait_recv()

    y_at = {off: wrap(y + off, NY) for off in (0, 1, -1, 2)}
    xp, xm = wrap(x + 1, NX), wrap(x - 1, NX)
    x2 = wrap(x + 2, NX)
    zp, zm = wrap(z + 1, NZ), wrap(z - 1, NZ)

    load_cot = pltpu.make_async_copy(cot_h, cot, loc.at[9])
    load_ctx = pltpu.make_async_copy(ctx_h, ctx, loc.at[10])
    load_cot.start()
    load_ctx.start()
    stats = [
        pltpu.make_async_copy(a, b, loc.at[i])
        for i, (a, b) in enumerate(((rl, rl_v), (rr, rr_v), (sm, sm_v), (ls, ls_v), (rs, rs_v)))
    ]

    barrier = pltpu.get_barrier_semaphore()
    near = [{"y": y_at[off]} for off in PEER_OFF] + [{"x": xp}, {"x": xm}, {"x": x2}, {"z": zp}, {"z": zm}, {"c": 1 - c}]
    for where in near:
        pl.semaphore_signal(barrier, inc=1, device_id=where, device_id_type=MESH)

    src_col = lax.broadcasted_iota(jnp.int32, (512, 512), 0)
    q = lax.broadcasted_iota(jnp.int32, (512, 512), 1)
    lane = lax.rem(q, 128)
    y_of = lax.rem(q // 128 + y, NY)
    pick = (src_col == (lane // PATCH) * BLOCK + PATCH * y_of + lax.rem(lane, PATCH)).astype(f32).astype(bf16)
    load_cot.wait()
    for j in range(2):
        got = jnp.dot(cot[:, 512 * j : 512 * j + 512], pick, preferred_element_type=f32).astype(bf16)
        for r in range(NY):
            pieces[r, :, 128 * j : 128 * j + 128] = got[:, 128 * r : 128 * r + 128]

    def bpart(t, ya, half=None):
        if half is None:
            return bq.at[t, pl.ds(ya * TOK, TOK)]
        return bq.at[t, pl.ds(ya * TOK + half * (TOK // 2), TOK // 2)]

    pl.semaphore_wait(barrier, len(near))

    here = bpart(t_me, y)
    send(pieces.at[1], here, ("By", -1), y=y_at[1])
    send(pieces.at[3], here, ("By", 1), y=y_at[-1])
    send(pieces.at[0], here, ("Bx", -1, 0), x=xp)
    send(pieces.at[0], here, ("Bx", 1, 0), x=xm)
    send(pieces.at[0], here, ("Bc", 0, 0), c=1 - c)
    send(pieces.at[0], here, ("Bx2", 0, 0), x=x2)
    for copy in stats:
        copy.start()

    load_ctx.wait()
    turn[...] = ctx[...].astype(f32).T.astype(bf16)
    lanes = pl.ds(pl.multiple_of(y * TOK, TOK), TOK)
    for pos, rel in enumerate(REL):
        zz = wrap(z + rel, NZ)
        for h in range(2):
            aall[pos * 64 + h * 32 : pos * 64 + h * 32 + 32, lanes] = turn[
                pl.ds(pl.multiple_of(h * 256 + zz * 32, 32), 32)
            ]

    def apart(off, k):
        first, end = SETS[k]
        return aall.at[pl.ds(first, end - first), pl.ds(pl.multiple_of(y_at[off] * TOK, TOK), TOK)]

    def send_rows(k):
        for off in PEER_OFF:
            send(apart(0, k), apart(0, k), ("A", k, -off if off != 2 else 2), y=y_at[off])

    send_rows(0)
    send(pieces.at[2], here, ("By", 2), y=y_at[2])
    for k in range(1, len(SETS)):
        send_rows(k)
    bq[t_me, pl.ds(y * TOK, TOK)] = pieces[0]

    def spread(yi):
        part = bpart(t_me, y_at[Y_OFF[yi]])
        arrived(part, "By", Y_OFF[yi])
        send(part, part, ("Bx", -1, yi), x=xp)
        send(part, part, ("Bx", 1, yi), x=xm)
        send(part, part, ("Bc", 0, yi), c=1 - c)

    def pass_on(yi):
        ya = y_at[Y_OFF[yi]]
        for off, x_at, half, to in ((-1, xm, 0, xp), (1, xp, 1, xm)):
            t = x_at * 2 + c
            arrived(bpart(t, ya), "Bx", off, yi)
            if yi:
                send(bpart(t, ya, half), bpart(t, ya, half), ("Bx2", half, yi), x=to)
            send(bpart(t, ya), bpart(t, ya), ("Bc", off, yi), c=1 - c)

    def far(yi):
        t = wrap(x + 2, NX) * 2 + c
        ya = y_at[Y_OFF[yi]]
        if yi:
            arrived(bpart(t, ya, 0), "Bx2", 0, yi)
            arrived(bpart(t, ya, 1), "Bx2", 1, yi)
        else:
            arrived(bpart(t, ya), "Bx2", 0, 0)
        send(bpart(t, ya), bpart(t, ya), ("Bc", 2, yi), c=1 - c)

    def rows_here(k):
        for off in PEER_OFF:
            arrived(apart(off, k), "A", k, off)

    def columns_here(u):
        if u % 2:
            for yi in range(NY):
                arrived(here, "Bc", X_OFF[u // 2], yi)

    def piece_of(u):
        xa = wrap(x + X_OFF[u // 2], NX)
        return xa * 2 + (1 - c if u % 2 else c)

    def product(u, k, end=None):
        first = SETS[k][0]
        last_row = SETS[k if end is None else end][1]
        total = jnp.dot(aall[first:last_row], bq[piece_of(u)], preferred_element_type=f32)
        cbuf[u, first // 64 : last_row // 64] = total.astype(bf16).reshape((last_row - first) // 64, 64, QC)

    def step(u, s):
        for d, to in ((0, zp), (1, zm)):
            name = ("Z", u, d, s)
            half = pl.ds(32 * d, 32)
            if s == 1:
                send(cbuf.at[u, 0, half], zr.at[u, d, 0, half], name, z=to)
                continue
            pos = 2 * s - 3 + d
            if s == 2:
                arrived(zr.at[u, d, 0, half], "Z", u, d, 1)
                cbuf[u, pos, half] = (cbuf[u, pos, half].astype(f32) + zr[u, d, 0, half].astype(f32)).astype(bf16)
            else:
                arrived(zr.at[u, d, s - 2], "Z", u, d, s - 1)
                cbuf[u, pos] = (cbuf[u, pos].astype(f32) + zr[u, d, s - 2].astype(f32)).astype(bf16)
            send(cbuf.at[u, pos], zr.at[u, d, s - 1], name, z=to)

    def last(u):
        arrived(zr.at[u, 0, 3], "Z", u, 0, 4)
        arrived(zr.at[u, 1, 3], "Z", u, 1, 4)
        whole = cbuf[u, 7].astype(f32) + zr[u, 0, 3].astype(f32) + zr[u, 1, 3].astype(f32)
        for j in range(2):
            tile = whole[:, 128 * j : 128 * j + 128]
            summed[piece_of(u) * 2 + j, 0] = tile[:32]
            summed[piece_of(u) * 2 + j, 1] = tile[32:]

    def steps(*pairs):
        for u, s in pairs:
            step(u, s)

    spread(1)
    spread(2)
    pass_on(0)
    rows_here(0)
    spread(3)
    product(0, 0)
    step(0, 1)
    columns_here(1)
    product(1, 0)
    step(1, 1)
    pass_on(1)
    pass_on(2)
    far(0)
    rows_here(1)
    for u in (0, 1):
        product(u, 1)
        step(u, 2)
    rows_here(2)
    for u in (0, 1):
        product(u, 2)
        step(u, 3)
    pass_on(3)
    for u in (2, 4, 3, 5):
        columns_here(u)
        product(u, 0, 2)
        step(u, 1)
    rows_here(3)
    for u in (0, 1):
        product(u, 3)
        step(u, 4)
    far(1)
    far(2)
    for u in (2, 4, 3, 5):
        product(u, 3)
        step(u, 2)
    far(3)
    for u in (6, 7):
        columns_here(u)
        product(u, 0, 3)
        step(u, 1)
    steps((2, 3), (4, 3), (3, 3), (5, 3))
    last(0)
    last(1)
    steps((6, 2), (7, 2), (2, 4), (4, 4), (6, 3), (7, 3), (3, 4), (5, 4), (6, 4), (7, 4))
    for u in (2, 4, 3, 5, 6, 7):
        last(u)

    left_lanes = lax.broadcasted_iota(jnp.int32, (16, 128), 1) < 64

    def patch(f, s):
        k = tbl[0, 2 * f + s]
        col = k & 31
        tile = summed[col >> 1, k >> 5]
        odd = (col & 1) == 1
        upper, lower = tile[:16], tile[16:]
        first = jnp.where(odd, pltpu.roll(upper, 64, 1), upper)
        second = jnp.where(odd, lower, pltpu.roll(lower, 64, 1))
        return jnp.where(left_lanes, first, second).astype(bf16)

    def other(i):
        k = i // NY
        dz = 4 + ((k + 1) // 2) * (1 - 2 * lax.rem(k, 2))
        zd = lax.rem(z + dz, NZ)
        yd = lax.rem(y + 3 - lax.rem(i, NY), NY)
        return zd, yd, zd * NY + yd

    def copy1(i, s):
        zd, yd, f = other(i)
        return pltpu.make_async_remote_copy(
            src_ref=out1.at[s, i], dst_ref=in1.at[s, me], send_sem=a1s.at[s, i], recv_sem=a1r.at[s, i],
            device_id={"z": zd, "y": yd}, device_id_type=MESH,
        )

    def copy2(i, s):
        zd, yd, f = other(i)
        return pltpu.make_async_remote_copy(
            src_ref=dirs.at[s, lax.rem(f, 16)], dst_ref=in2.at[s, me], send_sem=a2s.at[s, i], recv_sem=a2r.at[s, i],
            device_id={"z": zd, "y": yd}, device_id_type=MESH,
        )

    def each(do):
        def body(k, carry):
            for i in range(NY):
                do(k * NY + i)
            return carry

        lax.fori_loop(0, NZ - 1, body, 0)
        for i in range(NY * (NZ - 1), NY * NZ - 1):
            do(i)

    for s in range(2):

        def send1(k, carry, s=s, dests=NY):
            for i in range(dests):
                out1[s, k * NY + i] = patch(other(k * NY + i)[2], s)
            for i in range(dests):
                copy1(k * NY + i, s).start()
            return carry

        lax.fori_loop(0, NZ - 1, send1, 0)
        send1(NZ - 1, 0, dests=NY - 1)
        in1[s, me] = patch(me, s)

    highest = lax.Precision.HIGHEST
    for copy in stats[:3]:
        copy.wait()
    out_sn = []
    for s in range(2):
        each(lambda i, s=s: copy1(i, s).wait_recv())
        for j in range(2):
            for zz in range(NZ):
                a = in1[s, zz * NY + 2 * j].astype(f32)
                b = in1[s, zz * NY + 2 * j + 1].astype(f32)
                at = pl.ds(128 * j, 128)
                grad[s, 32 * zz : 32 * zz + 16, at] = jnp.where(left_lanes, a, pltpu.roll(b, 64, 1))
                grad[s, 32 * zz + 16 : 32 * zz + 32, at] = jnp.where(left_lanes, pltpu.roll(a, 64, 1), b)
        g = grad[s]
        second = decay_rate * sm_v[s] + (1.0 - decay_rate) * g * g
        sm_v[s] = second
        adam = g / (jnp.sqrt(second) + 1e-08)
        shaped = jnp.dot(rl_v[s], g, precision=highest, preferred_element_type=f32)
        shaped = jnp.dot(shaped, rr_v[s], precision=highest, preferred_element_type=f32)
        ratio = jnp.sqrt(jnp.sum(adam * adam, keepdims=True)) / jnp.sqrt(
            jnp.sum(shaped * shaped, keepdims=True) + 1e-06
        )
        dirs[s] = (shaped * ratio).astype(bf16).reshape(16, 16, BLOCK)
        each(lambda i, s=s: copy2(i, s).start())
        in2[s, me] = dirs[s, lax.rem(me, 16)]

    out_sn = pltpu.make_async_copy(sm_v, sn, loc.at[5])
    out_sn.start()
    for copy in stats[3:]:
        copy.wait()
    for s in range(2):
        g = grad[s].astype(bf16)
        left = lax.dot_general(g, g, (((1,), (1,)), ((), ())), preferred_element_type=f32)
        ls_v[s] = decay_rate * ls_v[s] + (1.0 - decay_rate) * left / BLOCK
        right = lax.dot_general(g, g, (((0,), (0,)), ((), ())), preferred_element_type=f32)
        rs_v[s] = decay_rate * rs_v[s] + (1.0 - decay_rate) * right / BLOCK
    out_ln = pltpu.make_async_copy(ls_v, ln, loc.at[6])
    out_rn = pltpu.make_async_copy(rs_v, rn, loc.at[7])
    out_ln.start()
    out_rn.start()

    for copy in started:
        copy.wait_send()
    for s in range(2):
        each(lambda i, s=s: copy1(i, s).wait_send())
    for s in range(2):
        each(lambda i, s=s: copy2(i, s).wait_recv())
    half = me // 16
    for col in range(32):
        p = inv[0, half * 32 + col]
        rows[:, BLOCK * col : BLOCK * col + BLOCK] = in2[p & 1, p >> 1]
    out_sd = pltpu.make_async_copy(rows, sd, loc.at[8])
    out_sd.start()
    for s in range(2):
        each(lambda i, s=s: copy2(i, s).wait_send())
    for copy in (out_sn, out_ln, out_rn, out_sd):
        copy.wait()


def emit(*refs):
    ins, outs, held, sems = refs[:4], refs[4:8], refs[8:12], refs[12]
    for i in range(4):
        pltpu.make_async_copy(ins[i], held[i], sems.at[i]).start()
    for i in range(4):
        pltpu.make_async_copy(ins[i], held[i], sems.at[i]).wait()
        pltpu.make_async_copy(held[i], outs[i], sems.at[i]).start()
    for i in range(4):
        pltpu.make_async_copy(held[i], outs[i], sems.at[i]).wait()


def per_device(context, cotangent, block_table, left_stat, right_stat, root_left, root_right, second_moment):
    ids = jnp.arange(64, dtype=jnp.int32)
    inverse = jnp.sum(jnp.where(block_table[0][None, :] == ids[:, None], ids[None, :], 0), axis=1)[None]
    smem = pl.BlockSpec(memory_space=pltpu.SMEM)
    hbm = pl.BlockSpec(memory_space=pltpu.HBM)
    block = jax.ShapeDtypeStruct((2, BLOCK, BLOCK), f32)
    V = pltpu.VMEM
    DMA = pltpu.SemaphoreType.DMA
    shapes = (block, block, block, jax.ShapeDtypeStruct((16, 8192), bf16))
    made = pl.pallas_call(
        kernel,
        out_shape=(block, block, block, jax.ShapeDtypeStruct((16, 8192), bf16)),
        in_specs=[hbm, hbm, smem, smem, hbm, hbm, hbm, hbm, hbm],
        out_specs=(hbm, hbm, hbm, hbm),
        scratch_shapes=[
            V((TOK, BAND), bf16),
            V((TOK, COLS), bf16),
            V((BAND, TOK), bf16),
            V((NY, TOK, QC), bf16),
            V((8, NY * TOK, QC), bf16),
            V((BAND, NY * TOK), bf16),
            V((8, NZ, 64, QC), bf16),
            V((8, 2, 4, 64, QC), bf16),
            V((16, 2, 32, 128), f32),
            V((2, 32, 16, 128), bf16),
            V((2, 32, 16, 128), bf16),
            V((2, BLOCK, BLOCK), f32),
            V((2, 16, 16, BLOCK), bf16),
            V((2, 32, 16, BLOCK), bf16),
            V((16, 8192), bf16),
            *[V((2, BLOCK, BLOCK), f32)] * 5,
            DMA((N_SEND,)),
            DMA((N_RECV,)),
            DMA((2, 32)),
            DMA((2, 32)),
            DMA((2, 32)),
            DMA((2, 32)),
            DMA((11,)),
        ],
        compiler_params=pltpu.CompilerParams(collective_id=0, has_side_effects=True, vmem_limit_bytes=67_043_328),
        name="shampoo",
    )(
        context, cotangent, block_table, inverse,
        left_stat[0], right_stat[0], root_left[0], root_right[0], second_moment[0],
    )
    ln, rn, sn, sd = pl.pallas_call(
        emit,
        out_shape=shapes,
        in_specs=[hbm] * 4,
        out_specs=(hbm,) * 4,
        scratch_shapes=[*[V(v.shape, v.dtype) for v in shapes], DMA((4,))],
        compiler_params=pltpu.CompilerParams(vmem_limit_bytes=67_043_328),
        name="emit",
    )(*made)
    return ln[None], rn[None], sn[None], sd[None]


def solution(mesh):
    finer = Mesh(mesh.devices.reshape(NZ, NY, NX, 2), ("z", "y", "x", "c"))
    F, T = ("z", "y"), ("x", "c")
    stat = P(T, F, None, None)
    return jax.shard_map(
        per_device,
        mesh=finer,
        in_specs=(P(F, T), P(F, T), P(T, None), stat, stat, stat, stat, stat),
        out_specs=(stat, stat, stat, P(T, F, None)),
        check_vma=False,
    )
```
